512 devices in a mesh: req: 64 (over x, z, core), wt: 8 (over y).
Axes of the slice: x: 4, y: 8, z: 8, core: 2. Of those that a mesh axis runs over, the one named last changes fastest.
Arguments:
- streams: bfloat16 [4, 32768, 2048], P(None, 'req', 'wt'), may hold values from -6 to 6
- doc_ids: int32 [64, 512], P('req'), may hold values from 0 to 3, never falling along the last dimension, each value on 1 to 256 neighbouring positions
- doc_adapter: int32 [64, 4, 1], P('req'), may hold values from 0 to 15
- width_weights: float32 [4], replicated, may hold values from 0.2 to 1
- stream_mixing: float32 [4, 4], replicated, may hold values from -3 to 3
- depth_static: float32 [4], replicated, may hold values from 0.2 to 1
- depth_dir: bfloat16 [2048, 4], replicated, may hold values from -0.125 to 0.125
- qkv_weight: bfloat16 [2048, 3, 2048], P('req', None, 'wt')
- adapter_down: bfloat16 [16, 2048, 16], P('wt'), may hold values from -0.125 to 0.125
- adapter_up: bfloat16 [16, 16, 3, 2048], P(None, None, None, 'wt'), may hold values from -1.5 to 1.5
- out_weight: bfloat16 [2048, 2048], P('req', 'wt'), may hold values from -0.125 to 0.125
- page_slot: int32 [2048], P('req'), may hold values from 0 to 2047, as said below
Outputs:
- new_streams: bfloat16 [4, 32768, 2048], P(None, 'req', 'wt')
- kv_pool: bfloat16 [2048, 16, 2, 2048], P('req', None, None, 'wt')
The draws below stay inside these ranges and needn't reach their ends.
Inputs may be any that keep to these rules, and one draw needn't show every extreme that they name: page_slot is a permutation of all page slots; page p lands on index page_slot[p] // 32 of req; the pages 2k and 2k + 1 form one request and land on the same index; of the pages of one index of req at most 2 land on any one index, and exactly 2 on some.
All inputs are finite; a program needn't handle non-finite values.
Results may differ from the reference program's by a relative error of at most 0.008.
Values may be sent and summed in bfloat16 or wider, within the bound.
A program may use at most 64 MiB of HBM per device.

```python
import math
import jax
import jax.numpy as jnp
import numpy as np
from jax import lax

D = 2048
H = 16
HD = 128
STREAMS = 4
R = 16
DOC_DEV = 4
PAGE = 16
TOK_DEV = 512
REQ_GROUPS = 64
TOKENS = 32768
ADAPTERS = 16
PAGES_DEV = 32
PAGES = 2048


def draw_qkv_weight(key, part):
    base = jax.random.truncated_normal(key, -4.0, 4.0, (D, 3, H * HD), jnp.float32) * D ** (-0.5)
    return base.astype(jnp.bfloat16)


def draw_page_slot(key, part):
    groups = REQ_GROUPS
    per_device = PAGES_DEV
    pairs = per_device // 2
    subkeys = jax.random.split(key, 4)
    device_order = jax.random.permutation(subkeys[0], groups)
    repeats = (pairs + groups - 1) // groups
    offset_list = jnp.concatenate([jax.random.permutation(jax.random.fold_in(subkeys[1], index), groups) for index in range(repeats)])[:pairs]
    source_order = jax.vmap(lambda subkey: jax.random.permutation(subkey, pairs))(jax.random.split(subkeys[2], groups))
    arrival_order = jax.vmap(lambda subkey: jax.random.permutation(subkey, pairs))(jax.random.split(subkeys[3], groups))
    target_dev = (device_order[:, None] + offset_list[source_order]) % groups
    pair_slot = arrival_order[target_dev, source_order]
    halves = jnp.arange(2, dtype=jnp.int32)
    local_slot = 2 * pair_slot[:, :, None] + halves[None, None, :]
    full_target = jnp.broadcast_to(target_dev[:, :, None], local_slot.shape)
    return (full_target * per_device + local_slot).reshape(-1).astype(jnp.int32)


def shard_levels(own_key, shape, pieces, least, top_value):
    def one(dim, blocks):
        steps = jax.random.uniform(jax.random.fold_in(jax.random.fold_in(own_key, 6), dim), (blocks,), jnp.float32, least / len(pieces), top_value / len(pieces))
        return jnp.repeat(jnp.exp(steps), shape[dim] // blocks).reshape((-1,) + (1,) * (len(shape) - dim - 1))

    level = one(*pieces[0])
    for cut in pieces[1:]:
        level = level * one(*cut)
    return level


def choose_distinct(own_key, rows, number_of, top, lift):
    ranking = jax.random.permutation(jax.random.fold_in(own_key, 1), number_of)
    favour = ranking
    for power in range(3):
        favour = favour * favour // number_of
    favour = favour * lift // number_of
    lots = jax.random.randint(jax.random.fold_in(own_key, 2), (rows, number_of), 0, 4096) + favour
    sure = jax.random.permutation(jax.random.fold_in(own_key, 3), rows)[jnp.arange(number_of) % rows]
    lots = jnp.where(jnp.arange(rows)[:, None] == sure[None, :], 1 << 14, lots)
    score = lots * number_of + jnp.arange(number_of)
    return lax.top_k(score.astype(jnp.int32), top)[1].astype(jnp.int32)


def profile(count, total, most, skew):
    loads = [(1 << 20) // math.isqrt(standing ** skew) + 1 for standing in range(2, count + 1)]
    spare, counts = total - most - (count - 1), [1] * (count - 1)
    while spare > 0:
        candidates = [i for i in range(count - 1) if counts[i] < most]
        pool, remaining = sum([loads[i] for i in candidates]), spare
        for i in candidates:
            addition = min(most - counts[i], max(1, remaining * loads[i] // pool), spare)
            counts[i] = counts[i] + addition
            spare = spare - addition
    return np.array([most] + counts)


def uneven(rng, count, total, reach, slope):
    if count == 2:
        one = jax.random.randint(rng, (), max(1, total - reach), min(reach, total - 1) + 1)
        return jnp.stack([one, total - one])
    tallies = jnp.asarray(profile(count, total, reach, slope), jnp.int32)
    couples = (count - 1) // 2
    giver, receiver = tallies[1:1 + 2 * couples:2], tallies[2:2 + 2 * couples:2]
    margin = jnp.minimum(giver - 1, reach - receiver)
    shifted = jax.random.randint(jax.random.fold_in(rng, 1), (couples,), 0, 1 << 20) % (margin + 1)
    tallies = tallies.at[1:1 + 2 * couples:2].set(giver - shifted).at[2:2 + 2 * couples:2].set(receiver + shifted)
    return tallies[jax.random.permutation(jax.random.fold_in(rng, 2), count)]


def normal_values(stream_key, extent, scale, most, cuts=(), kind=jnp.bfloat16):
    result = jax.random.normal(stream_key, extent, jnp.float32) * scale
    if len(cuts) > 0:
        result = shard_levels(stream_key, extent, cuts, -0.22, 0.18) * result
    return jnp.clip(result, min=-most, max=most).astype(kind)


def setup_inputs(seed: int = 0) -> dict:
    key_list = jax.random.split(jax.random.key(seed), 13)
    streams = normal_values(key_list[0], (STREAMS, TOKENS, D), 1.0, 6.0, ((1, 64), (2, 8)))
    doc_ids = jax.vmap(lambda own: jnp.searchsorted(jnp.cumsum(uneven(own, DOC_DEV, TOK_DEV, TOK_DEV // 2, 2)), jnp.arange(TOK_DEV), side="right"))(jax.random.split(key_list[1], REQ_GROUPS)).reshape((REQ_GROUPS, TOK_DEV)).astype(jnp.int32)
    doc_adapter = choose_distinct(key_list[2], REQ_GROUPS * DOC_DEV, ADAPTERS, 1, 1024).reshape((REQ_GROUPS, DOC_DEV, 1))
    width_weights = jnp.clip(jax.random.uniform(key_list[3], (STREAMS,), jnp.float32, 0.2, 1.0), 0.2, 1.0)
    stream_mixing = normal_values(key_list[4], (STREAMS, STREAMS), 0.5, 3.0, (), jnp.float32)
    depth_static = jnp.clip(jax.random.uniform(key_list[5], (STREAMS,), jnp.float32, 0.2, 1.0), 0.2, 1.0)
    depth_dir = normal_values(key_list[6], (D, STREAMS), D ** -0.5, 0.125)
    qkv_weight = draw_qkv_weight(jax.random.fold_in(key_list[12], 71), 0)
    adapter_down = normal_values(key_list[8], (ADAPTERS, D, R), D ** -0.5, 0.125, ((0, 8),))
    adapter_up = normal_values(key_list[9], (ADAPTERS, R, 3, H * HD), R ** -0.5, 1.5, ((3, 8),))
    out_weight = normal_values(key_list[10], (H * HD, D), (H * HD) ** -0.5, 0.125, ((0, 64), (1, 8)))
    page_slot = draw_page_slot(jax.random.fold_in(key_list[12], 71), 0)
    return {"streams": streams, "doc_ids": doc_ids, "doc_adapter": doc_adapter, "width_weights": width_weights, "stream_mixing": stream_mixing, "depth_static": depth_static, "depth_dir": depth_dir, "qkv_weight": qkv_weight, "adapter_down": adapter_down, "adapter_up": adapter_up, "out_weight": out_weight, "page_slot": page_slot}


EPSILON = 1e-05

def attend_block(packed):
    query_rows, key_rows, value_rows, segment = packed
    scores = jnp.einsum('qhd,khd->hqk', query_rows.astype(jnp.float32), key_rows.astype(jnp.float32)) / math.sqrt(HD)
    positions = jnp.arange(segment.shape[0])
    allowed = (segment[:, None] == segment[None, :]) & (positions[None, :] <= positions[:, None])
    scores = jnp.where(allowed[None], scores, -1e+30)
    highest = lax.optimization_barrier(jnp.max(scores, axis=-1, keepdims=True))
    weights = jnp.exp(scores - highest)
    weights = (weights / lax.optimization_barrier(jnp.sum(weights, axis=-1, keepdims=True))).astype(jnp.bfloat16)
    return jnp.einsum('hqk,khd->qhd', weights.astype(jnp.float32), value_rows.astype(jnp.float32)).astype(jnp.bfloat16)

def reference(streams, doc_ids, doc_adapter, width_weights, stream_mixing, depth_static, depth_dir, qkv_weight, adapter_down, adapter_up, out_weight, page_slot):
    mixed_in = width_weights[0] * streams[0].astype(jnp.float32)
    for stream in range(1, STREAMS):
        mixed_in = mixed_in + width_weights[stream] * streams[stream].astype(jnp.float32)
    widened = mixed_in.astype(jnp.bfloat16).astype(jnp.float32)
    normed = (widened * lax.rsqrt(lax.optimization_barrier(jnp.mean(widened * widened, axis=-1, keepdims=True)) + EPSILON)).astype(jnp.bfloat16)
    token_adapter = jnp.take_along_axis(doc_adapter[:, :, 0], doc_ids, axis=1).reshape(-1)
    selector = (token_adapter[:, None] == jnp.arange(ADAPTERS)[None, :]).astype(jnp.float32)
    every_rank = jnp.einsum('td,adr->tar', normed.astype(jnp.float32), adapter_down.astype(jnp.float32))
    shrunk = lax.optimization_barrier(jnp.sum(selector[:, :, None] * every_rank, axis=1)).astype(jnp.bfloat16)
    spread = (selector[:, :, None] * shrunk.astype(jnp.float32)[:, None, :]).reshape(TOKENS, ADAPTERS * R).astype(jnp.bfloat16)
    lowrank = jnp.dot(spread, adapter_up.reshape(ADAPTERS * R, 3 * H * HD), preferred_element_type=jnp.float32)
    base = jnp.dot(normed, qkv_weight.reshape(D, 3 * H * HD), preferred_element_type=jnp.float32)
    projected = (base + lowrank).astype(jnp.bfloat16).reshape(REQ_GROUPS, TOK_DEV, 3, H, HD)
    attended = lax.map(attend_block, (projected[:, :, 0], projected[:, :, 1], projected[:, :, 2], doc_ids))
    attended = attended.reshape(TOKENS, H * HD)
    layer_out = jnp.dot(attended, out_weight, preferred_element_type=jnp.float32)
    depth = depth_static[None, :] + jnp.tanh(jnp.dot(normed, depth_dir, preferred_element_type=jnp.float32))
    outputs = []
    for stream in range(STREAMS):
        carried = stream_mixing[stream, 0] * streams[0].astype(jnp.float32)
        for source in range(1, STREAMS):
            carried = carried + stream_mixing[stream, source] * streams[source].astype(jnp.float32)
        outputs.append((carried + depth[:, stream][:, None] * layer_out).astype(jnp.bfloat16))
    new_streams = jnp.stack(outputs)
    cache = projected[:, :, 1:3].reshape(PAGES, PAGE, 2, H * HD)
    kv_pool = jnp.zeros((PAGES, PAGE, 2, H * HD), jnp.bfloat16).at[page_slot].set(cache)
    return (new_streams, kv_pool)
```

```python
import functools
import math

import jax
import jax.numpy as jnp
from jax import lax
from jax.experimental import pallas as pl
from jax.experimental.pallas import tpu as pltpu
from jax.sharding import PartitionSpec as P

HD = 128
R = 16
PAGE = 16
NX, NZ, NC, NY = 4, 8, 2, 8

EPSILON = 1e-05
MESH = pl.DeviceIdType.MESH


class Copies:
    def __init__(self, send_sem, recv_sem):
        self.send_sem, self.recv_sem = send_sem, recv_sem
        self.count = 0
        self.started = []

    def start(self, src, dst, req, wt):
        index = self.count
        self.count += 1
        copy = pltpu.make_async_remote_copy(
            src_ref=src,
            dst_ref=dst,
            send_sem=self.send_sem.at[index],
            recv_sem=self.recv_sem.at[index],
            device_id=(req, wt),
            device_id_type=MESH,
        )
        copy.start()
        self.started.append(copy)
        return copy

    def finish(self):
        for copy in self.started:
            copy.wait_send()


def position():
    req = lax.axis_index("req")
    wt = lax.axis_index("wt")
    core = lax.rem(req, NC)
    z = lax.rem(req // NC, NZ)
    x = req // (NC * NZ)
    return req, wt, x, z, core


def turn(value, shift, size):
    return lax.rem(value + (shift + size), size)


def meet(partners):
    barrier = pltpu.get_barrier_semaphore()
    for req, wt in partners:
        pl.semaphore_signal(barrier, inc=1, device_id=(req, wt), device_id_type=MESH)
    pl.semaphore_wait(barrier, len(partners))


def columns(ref, half, origin):
    rows = ref.shape[0] // 2
    width = ref.shape[1] // NY
    return ref.at[pl.ds(half * rows, rows), pl.ds(pl.multiple_of(origin * width, width), width)]


def token_hop(copies, held, own, out, req, wt, half, direction, step):
    if step == 3 and half != (0 if direction == 1 else 1):
        return
    key = (half, direction)
    if step > 0:
        held[key].wait_recv()
    origin = turn(wt, -direction * step, NY)
    rows = out.shape[0] // 2
    src = own.at[pl.ds(half * rows, rows)] if step == 0 else columns(out, half, origin)
    held[key] = copies.start(src, columns(out, half, origin), req, turn(wt, direction, NY))


def gather_kernel(mixed, rows, down, mixed_all, rows_all, down_all, send_sem, recv_sem, local_sem):
    req, wt, x, z, core = position()
    partner = req + 1 - 2 * core

    def at(x_at, z_at):
        return (x_at * NZ + z_at) * NC + core

    def near_x(shift):
        return at(turn(x, shift, NX), z)

    def near_z(shift):
        return at(x, turn(z, shift, NZ))

    meet(
        [(req, turn(wt, 1, NY)), (req, turn(wt, -1, NY)), (partner, wt)]
        + [(near_x(1), wt), (near_x(-1), wt), (near_z(1), wt), (near_z(-1), wt)]
    )
    copies = Copies(send_sem, recv_sem)
    held_tokens, held_down, held_rows = {}, {}, {}

    def rows_hop(unit, direction, step):
        if step == 3 and unit % 2 != (0 if direction == 1 else 1):
            return
        key = (unit, direction)
        if step > 0:
            held_rows[key].wait_recv()
        block = rows_all.at[turn(x, -unit, NX), turn(z, -direction * step, NZ), core]
        src = rows if (step == 0 and unit == 0) else block
        held_rows[key] = copies.start(src, block, near_z(direction), wt)

    def down_hop(direction, step):
        if step == 3 and direction == -1:
            return
        if step > 0:
            held_down[direction].wait_recv()
        block = down_all.at[turn(wt, -direction * step, NY), core]
        src = down.at[core] if step == 0 else block
        held_down[direction] = copies.start(src, block, req, turn(wt, direction, NY))

    def share(z_shift):
        block = rows_all.at[:, turn(z, z_shift, NZ), core]
        return copies.start(block, block, partner, wt)

    own_rows = rows_all.at[x, z, core]
    from_left = copies.start(rows, own_rows, near_x(1), wt)
    from_right = copies.start(rows, own_rows, near_x(-1), wt)
    for direction in (1, -1):
        token_hop(copies, held_tokens, mixed, mixed_all, req, wt, 0, direction, 0)
        rows_hop(0, direction, 0)
    for direction in (1, -1):
        token_hop(copies, held_tokens, mixed, mixed_all, req, wt, 1, direction, 0)
        down_hop(direction, 0)
    locals_ = [
        pltpu.make_async_copy(rows, own_rows, local_sem.at[0]),
        pltpu.make_async_copy(mixed.at[pl.ds(0, mixed.shape[0] // 2)], columns(mixed_all, 0, wt), local_sem.at[1]),
        pltpu.make_async_copy(
            mixed.at[pl.ds(mixed.shape[0] // 2, mixed.shape[0] // 2)], columns(mixed_all, 1, wt), local_sem.at[2]
        ),
        pltpu.make_async_copy(down.at[core], down_all.at[wt, core], local_sem.at[3]),
    ]
    for copy in locals_:
        copy.start()
    from_left.wait_recv()
    left_block = rows_all.at[turn(x, -1, NX), z, core]
    far = copies.start(left_block, left_block, near_x(1), wt)
    for direction in (1, -1):
        rows_hop(1, direction, 0)
    from_right.wait_recv()
    for direction in (1, -1):
        rows_hop(3, direction, 0)
    far.wait_recv()
    for direction in (1, -1):
        rows_hop(2, direction, 0)
    for copy in locals_:
        copy.wait()
    shared = [share(0)]
    for step in range(1, 4):
        for unit in (0, 1, 3, 2):
            for direction in (1, -1):
                rows_hop(unit, direction, step)
            if unit == 1 or unit == 2:
                for direction in (1, -1):
                    token_hop(
                        copies, held_tokens, mixed, mixed_all, req, wt, 0 if unit == 1 else 1, direction, step
                    )
        if step == 3:
            for unit in (1, 3):
                held_rows[(unit, 1)].wait_recv()
            for unit in (0, 2):
                held_rows[(unit, -1)].wait_recv()
        for direction in (1, -1):
            down_hop(direction, step)
        shared += [share(-step), share(step)]
    held_down[-1].wait_recv()
    held_down[1].wait_recv()
    every_down = down_all.at[:, core]
    shared.append(copies.start(every_down, every_down, partner, wt))
    for unit in (0, 2):
        held_rows[(unit, 1)].wait_recv()
    for unit in (1, 3):
        held_rows[(unit, -1)].wait_recv()
    shared.append(share(4))
    for half in (0, 1):
        for direction in (1, -1):
            held_tokens[(half, direction)].wait_recv()
    for copy in shared:
        copy.wait_recv()
    copies.finish()


def tokens_kernel(own, out, send_sem, recv_sem, local_sem):
    req, wt, _, _, _ = position()
    meet([(req, turn(wt, 1, NY)), (req, turn(wt, -1, NY))])
    copies = Copies(send_sem, recv_sem)
    held = {}
    rows = own.shape[0] // 2
    locals_ = []
    for step in range(4):
        for half in (0, 1):
            for direction in (1, -1):
                token_hop(copies, held, own, out, req, wt, half, direction, step)
            if step == 0:
                locals_.append(
                    pltpu.make_async_copy(own.at[pl.ds(half * rows, rows)], columns(out, half, wt), local_sem.at[half])
                )
                locals_[-1].start()
    for half in (0, 1):
        for direction in (1, -1):
            held[(half, direction)].wait_recv()
    for copy in locals_:
        copy.wait()
    copies.finish()


def spec(space):
    return pl.BlockSpec(memory_space=space)


def gather_all(mixed, rows, down):
    tokens, width = mixed.shape
    count = 3 + 28 + 8 + 14 + 7 + 1
    return pl.pallas_call(
        gather_kernel,
        out_shape=[
            jax.ShapeDtypeStruct((tokens, width * NY), mixed.dtype),
            jax.ShapeDtypeStruct((NX, NZ, NC) + rows.shape, rows.dtype),
            jax.ShapeDtypeStruct((NY,) + down.shape, down.dtype),
        ],
        in_specs=[spec(pltpu.VMEM)] * 3,
        out_specs=[spec(pl.ANY)] * 3,
        scratch_shapes=[
            pltpu.SemaphoreType.DMA((count,)),
            pltpu.SemaphoreType.DMA((count,)),
            pltpu.SemaphoreType.DMA((4,)),
        ],
        compiler_params=pltpu.CompilerParams(collective_id=0, has_side_effects=True),
    )(mixed, rows, down)


def gather_tokens(own):
    tokens, width = own.shape
    return pl.pallas_call(
        tokens_kernel,
        out_shape=jax.ShapeDtypeStruct((tokens, width * NY), own.dtype),
        in_specs=[spec(pltpu.VMEM)],
        out_specs=spec(pl.ANY),
        scratch_shapes=[
            pltpu.SemaphoreType.DMA((14,)),
            pltpu.SemaphoreType.DMA((14,)),
            pltpu.SemaphoreType.DMA((2,)),
        ],
        compiler_params=pltpu.CompilerParams(collective_id=1, has_side_effects=True),
        cost_estimate=pl.CostEstimate(flops=0, bytes_accessed=60_000_000, transcendentals=0),
    )(own)


def body(
    streams,
    doc_ids,
    doc_adapter,
    width_weights,
    stream_mixing,
    depth_static,
    depth_dir,
    qkv_weight,
    adapter_down,
    adapter_up,
    out_weight,
    page_slot,
):
    count_streams = streams.shape[0]
    tokens = streams.shape[1]
    mixed_local = width_weights[0] * streams[0].astype(jnp.float32)
    for stream in range(1, count_streams):
        mixed_local = mixed_local + width_weights[stream] * streams[stream].astype(jnp.float32)

    page_count = page_slot.shape[0]
    width_local = qkv_weight.shape[2]
    rows_local = qkv_weight.shape[0]
    groups = lax.axis_size("req")
    target_dev = page_slot // page_count
    local_slot = page_slot % page_count
    lane = jnp.arange(128)[None, :]
    labels = jnp.where(
        lane == 0, target_dev[:, None], jnp.where(lane == 1, local_slot[:, None], 0)
    ).astype(jnp.bfloat16)
    rows = jnp.concatenate([qkv_weight.reshape(rows_local, 3 * width_local), out_weight, labels], axis=1)
    gathered, rows_all, down_all = gather_all(
        mixed_local.astype(jnp.bfloat16), rows, adapter_down.transpose(0, 2, 1)
    )
    rows_all = rows_all.reshape(groups * rows_local, -1)
    qkv_all = rows_all[:, : 3 * width_local]
    out_all = rows_all[:, 3 * width_local : 4 * width_local]
    label_all = rows_all[:, 4 * width_local : 4 * width_local + 2].astype(jnp.int32)

    widened = gathered.astype(jnp.float32)
    normed = (
        widened * lax.rsqrt(jnp.mean(widened * widened, axis=-1, keepdims=True) + EPSILON)
    ).astype(jnp.bfloat16)
    segment = doc_ids[0]
    doc_table = doc_adapter[0, :, 0]
    token_adapter = jnp.sum(
        jnp.where(
            segment[:, None] == jnp.arange(doc_table.shape[0])[None, :], doc_table[None, :], 0
        ),
        axis=1,
    )
    adapters_total = adapter_up.shape[0]
    lanes = jnp.arange(adapters_total * R)[None, :]
    own_lane = token_adapter[:, None] == lanes // R
    every_rank = lax.dot_general(
        normed,
        down_all.reshape(adapters_total * R, -1),
        (((1,), (1,)), ((), ())),
        preferred_element_type=jnp.float32,
    )
    spread = jnp.where(own_lane, every_rank, 0.0).astype(jnp.bfloat16)
    lowrank = jnp.dot(
        spread, adapter_up.reshape(adapters_total * R, -1), preferred_element_type=jnp.float32
    )
    base = jnp.dot(normed, qkv_all, preferred_element_type=jnp.float32)
    heads_local = width_local // HD
    projected = (base + lowrank).astype(jnp.bfloat16)
    positions = jnp.arange(tokens)
    allowed = (segment[:, None] == segment[None, :]) & (positions[None, :] <= positions[:, None])
    parts = []
    for head in range(heads_local):
        query, key, value = (
            projected[:, part * width_local + head * HD : part * width_local + (head + 1) * HD]
            for part in range(3)
        )
        scores = lax.dot_general(
            query, key, (((1,), (1,)), ((), ())), preferred_element_type=jnp.float32
        ) / math.sqrt(HD)
        scores = jnp.where(allowed, scores, -1e30)
        highest = jnp.max(scores, axis=-1, keepdims=True)
        weights = jnp.exp(scores - highest)
        weights = (weights / jnp.sum(weights, axis=-1, keepdims=True)).astype(jnp.bfloat16)
        parts.append(jnp.dot(weights, value, preferred_element_type=jnp.float32).astype(jnp.bfloat16))
    attended = gather_tokens(jnp.concatenate(parts, axis=1))
    layer_out = jnp.dot(attended, out_all, preferred_element_type=jnp.float32)
    depth = depth_static[None, :] + jnp.tanh(
        jnp.dot(normed, depth_dir, preferred_element_type=jnp.float32)
    )
    outputs = []
    for stream in range(count_streams):
        carried = stream_mixing[stream, 0] * streams[0].astype(jnp.float32)
        for source in range(1, count_streams):
            carried = carried + stream_mixing[stream, source] * streams[source].astype(jnp.float32)
        outputs.append((carried + depth[:, stream][:, None] * layer_out).astype(jnp.bfloat16))
    new_streams = jnp.stack(outputs)

    cache = projected[:, width_local:].reshape(page_count, PAGE, 2, width_local)
    capacity = 2 * max(1, page_count // (2 * groups))
    ordinal = jnp.arange(page_count)
    earlier = (target_dev[None, :] == target_dev[:, None]) & (ordinal[None, :] < ordinal[:, None])
    placement = target_dev * capacity + jnp.sum(earlier.astype(jnp.int32), axis=1)
    outgoing = (
        jnp.zeros((groups * capacity, PAGE, 2, width_local), jnp.bfloat16).at[placement].set(cache)
    )
    incoming = lax.all_to_all(outgoing, "req", split_axis=0, concat_axis=0, tiled=True)
    came = (label_all[:, 0] == lax.axis_index("req")).reshape(groups, page_count)
    turn_in = jnp.cumsum(came.astype(jnp.int32), axis=1) - 1
    came_slot = label_all[:, 1].reshape(groups, page_count)
    slot_index = jnp.stack(
        [
            jnp.sum(jnp.where(came & (turn_in == number), came_slot + 1, 0), axis=1)
            for number in range(capacity)
        ],
        axis=1,
    ).reshape(-1)
    slot_index = jnp.where(slot_index == 0, page_count, slot_index - 1)
    kv_pool = (
        jnp.zeros((page_count + 1, PAGE, 2, width_local), jnp.bfloat16)
        .at[slot_index]
        .set(incoming)[:page_count]
    )
    return (new_streams, kv_pool)


def solution(mesh):
    in_specs = (
        P(None, "req", "wt"),
        P("req", None),
        P("req", None, None),
        P(),
        P(),
        P(),
        P(),
        P("req", None, "wt"),
        P("wt", None, None),
        P(None, None, None, "wt"),
        P("req", "wt"),
        P("req"),
    )
    out_specs = (P(None, "req", "wt"), P("req", None, None, "wt"))
    return jax.shard_map(body, mesh=mesh, in_specs=in_specs, out_specs=out_specs, check_vma=False)
```

```python
import functools
import math

import jax
import jax.numpy as jnp
from jax import lax
from jax.experimental import pallas as pl
from jax.experimental.pallas import tpu as pltpu
from jax.sharding import PartitionSpec as P

HD = 128
R = 16
PAGE = 16
NX, NZ, NC, NY = 4, 8, 2, 8

EPSILON = 1e-05
MESH = pl.DeviceIdType.MESH


class Copies:
    def __init__(self, send_sem, recv_sem):
        self.send_sem, self.recv_sem = send_sem, recv_sem
        self.count = 0
        self.started = []

    def start(self, src, dst, req, wt):
        index = self.count
        self.count += 1
        copy = pltpu.make_async_remote_copy(
            src_ref=src,
            dst_ref=dst,
            send_sem=self.send_sem.at[index],
            recv_sem=self.recv_sem.at[index],
            device_id=(req, wt),
            device_id_type=MESH,
        )
        copy.start()
        self.started.append(copy)
        return copy

    def finish(self):
        for copy in self.started:
            copy.wait_send()


def position():
    req = lax.axis_index("req")
    wt = lax.axis_index("wt")
    core = lax.rem(req, NC)
    z = lax.rem(req // NC, NZ)
    x = req // (NC * NZ)
    return req, wt, x, z, core


def turn(value, shift, size):
    return lax.rem(value + (shift + size), size)


def meet(partners):
    barrier = pltpu.get_barrier_semaphore()
    for req, wt in partners:
        pl.semaphore_signal(barrier, inc=1, device_id=(req, wt), device_id_type=MESH)
    pl.semaphore_wait(barrier, len(partners))


def columns(ref, half, origin):
    rows = ref.shape[0] // 2
    width = ref.shape[1] // NY
    return ref.at[pl.ds(half * rows, rows), pl.ds(pl.multiple_of(origin * width, width), width)]


def token_hop(copies, held, own, out, req, wt, half, direction, step):
    if step == 3 and half != (0 if direction == 1 else 1):
        return
    key = (half, direction)
    if step > 0:
        held[key].wait_recv()
    origin = turn(wt, -direction * step, NY)
    rows = out.shape[0] // 2
    src = own.at[pl.ds(half * rows, rows)] if step == 0 else columns(out, half, origin)
    held[key] = copies.start(src, columns(out, half, origin), req, turn(wt, direction, NY))


def gather_kernel(
    mixed, rows, out_rows, down, mixed_all, rows_all, out_all, down_all, send_sem, recv_sem, local_sem
):
    req, wt, x, z, core = position()
    partner = req + 1 - 2 * core

    def at(x_at, z_at):
        return (x_at * NZ + z_at) * NC + core

    def near_x(shift):
        return at(turn(x, shift, NX), z)

    def near_z(shift):
        return at(x, turn(z, shift, NZ))

    meet(
        [(req, turn(wt, 1, NY)), (req, turn(wt, -1, NY)), (partner, wt)]
        + [(near_x(1), wt), (near_x(-1), wt), (near_z(1), wt), (near_z(-1), wt)]
    )
    copies = Copies(send_sem, recv_sem)
    held_tokens, held_down, held_rows, held_out = {}, {}, {}, {}
    slice_width = down.shape[2] // NX

    def down_lanes(x_at):
        return pl.ds(pl.multiple_of(x_at * slice_width, slice_width), slice_width)

    def rows_hop(unit, direction, step):
        if step == 3 and unit % 2 != (0 if direction == 1 else 1):
            return
        key = (unit, direction)
        if step > 0:
            held_rows[key].wait_recv()
        block = rows_all.at[turn(x, -unit, NX), turn(z, -direction * step, NZ), core]
        src = rows if (step == 0 and unit == 0) else block
        held_rows[key] = copies.start(src, block, near_z(direction), wt)

    def token_step(half, step):
        for direction in (1, -1):
            token_hop(copies, held_tokens, mixed, mixed_all, req, wt, half, direction, step)

    def small_hop(step):
        for direction in (1, -1):
            if step == 3 and direction == -1:
                continue
            if step > 0:
                held_down[direction].wait_recv()
                held_out[direction].wait_recv()
            block = down_all.at[turn(wt, -direction * step, NY), core, :, down_lanes(x)]
            src = down.at[core, :, down_lanes(x)] if step == 0 else block
            held_down[direction] = copies.start(src, block, req, turn(wt, direction, NY))
            block = out_all.at[x, turn(z, -direction * step, NZ), core]
            src = out_rows if step == 0 else block
            held_out[direction] = copies.start(src, block, near_z(direction), wt)

    def small_blocks(shift):
        x_at = turn(x, shift, NX)
        return down_all.at[:, core, :, down_lanes(x_at)], out_all.at[x_at, :, core]

    def share(z_shift):
        block = rows_all.at[:, turn(z, z_shift, NZ), core]
        return copies.start(block, block, partner, wt)

    own_rows = rows_all.at[x, z, core]
    from_left = copies.start(rows, own_rows, near_x(1), wt)
    from_right = copies.start(rows, own_rows, near_x(-1), wt)
    small_hop(0)
    token_step(0, 0)
    for direction in (1, -1):
        rows_hop(0, direction, 0)
    token_step(1, 0)
    half = mixed.shape[0] // 2
    locals_ = [
        pltpu.make_async_copy(rows, own_rows, local_sem.at[0]),
        pltpu.make_async_copy(mixed.at[pl.ds(0, half)], columns(mixed_all, 0, wt), local_sem.at[1]),
        pltpu.make_async_copy(mixed.at[pl.ds(half, half)], columns(mixed_all, 1, wt), local_sem.at[2]),
        pltpu.make_async_copy(
            down.at[core, :, down_lanes(x)], down_all.at[wt, core, :, down_lanes(x)], local_sem.at[3]
        ),
        pltpu.make_async_copy(out_rows, out_all.at[x, z, core], local_sem.at[4]),
    ]
    for copy in locals_:
        copy.start()
    from_left.wait_recv()
    left_block = rows_all.at[turn(x, -1, NX), z, core]
    far = copies.start(left_block, left_block, near_x(1), wt)
    for direction in (1, -1):
        rows_hop(1, direction, 0)
    from_right.wait_recv()
    for direction in (1, -1):
        rows_hop(3, direction, 0)
    far.wait_recv()
    for direction in (1, -1):
        rows_hop(2, direction, 0)
    for copy in locals_:
        copy.wait()
    shared = [share(0)]
    small_left, small_right, small_far = [], [], []
    for step in range(1, 4):
        for unit in (0, 1, 3, 2):
            for direction in (1, -1):
                rows_hop(unit, direction, step)
            if unit == 1:
                token_step(0, step)
            if unit == 2:
                token_step(1, step)
            if (step, unit) == (1, 0):
                small_hop(1)
            if (step, unit) == (1, 3):
                small_hop(2)
            if (step, unit) == (2, 0):
                small_hop(3)
            if (step, unit) == (2, 3):
                for direction in (1, -1):
                    held_down[direction].wait_recv()
                    held_out[direction].wait_recv()
                for block in small_blocks(0):
                    small_left.append(copies.start(block, block, near_x(1), wt))
                    small_right.append(copies.start(block, block, near_x(-1), wt))
            if (step, unit) == (3, 0):
                for copy, block in zip(small_left, small_blocks(-1)):
                    copy.wait_recv()
                    small_far.append(copies.start(block, block, near_x(1), wt))
        if step == 3:
            for unit in (1, 3):
                held_rows[(unit, 1)].wait_recv()
            for unit in (0, 2):
                held_rows[(unit, -1)].wait_recv()
        shared += [share(-step), share(step)]
    for copy in small_right + small_far:
        copy.wait_recv()
    for block in (down_all.at[:, core], out_all.at[:, :, core]):
        shared.append(copies.start(block, block, partner, wt))
    for unit in (0, 2):
        held_rows[(unit, 1)].wait_recv()
    for unit in (1, 3):
        held_rows[(unit, -1)].wait_recv()
    shared.append(share(4))
    for half in (0, 1):
        for direction in (1, -1):
            held_tokens[(half, direction)].wait_recv()
    for copy in shared:
        copy.wait_recv()
    copies.finish()


def tokens_kernel(own, out, send_sem, recv_sem, local_sem):
    req, wt, _, _, _ = position()
    meet([(req, turn(wt, 1, NY)), (req, turn(wt, -1, NY))])
    copies = Copies(send_sem, recv_sem)
    held = {}
    rows = own.shape[0] // 2
    locals_ = []
    for step in range(4):
        for half in (0, 1):
            for direction in (1, -1):
                token_hop(copies, held, own, out, req, wt, half, direction, step)
            if step == 0:
                locals_.append(
                    pltpu.make_async_copy(own.at[pl.ds(half * rows, rows)], columns(out, half, wt), local_sem.at[half])
                )
                locals_[-1].start()
    for half in (0, 1):
        for direction in (1, -1):
            held[(half, direction)].wait_recv()
    for copy in locals_:
        copy.wait()
    copies.finish()


def spec(space):
    return pl.BlockSpec(memory_space=space)


def gather_all(mixed, rows, out_rows, down):
    tokens, width = mixed.shape
    count = 3 + 28 + 8 + 14 + 2 * (7 + 3 + 1)
    return pl.pallas_call(
        gather_kernel,
        out_shape=[
            jax.ShapeDtypeStruct((tokens, width * NY), mixed.dtype),
            jax.ShapeDtypeStruct((NX, NZ, NC) + rows.shape, rows.dtype),
            jax.ShapeDtypeStruct((NX, NZ, NC) + out_rows.shape, out_rows.dtype),
            jax.ShapeDtypeStruct((NY,) + down.shape, down.dtype),
        ],
        in_specs=[spec(pltpu.VMEM)] * 4,
        out_specs=[spec(pl.ANY)] * 4,
        scratch_shapes=[
            pltpu.SemaphoreType.DMA((count,)),
            pltpu.SemaphoreType.DMA((count,)),
            pltpu.SemaphoreType.DMA((5,)),
        ],
        compiler_params=pltpu.CompilerParams(collective_id=0, has_side_effects=True),
    )(mixed, rows, out_rows, down)


def mixed_kernel(weights, streams, out):
    total = weights[0] * streams[0].astype(jnp.float32)
    for stream in range(1, streams.shape[0]):
        total = total + weights[stream] * streams[stream].astype(jnp.float32)
    out[...] = total.astype(out.dtype)


def mix_in(width_weights, streams):
    count, tokens, width = streams.shape
    block = tokens // 2
    return pl.pallas_call(
        mixed_kernel,
        grid=(tokens // block,),
        out_shape=jax.ShapeDtypeStruct((tokens, width), streams.dtype),
        in_specs=[spec(pltpu.SMEM), pl.BlockSpec((count, block, width), lambda i: (0, i, 0))],
        out_specs=pl.BlockSpec((block, width), lambda i: (i, 0)),
    )(width_weights, streams)


def pack_kernel(placement, cache, out, sem):
    started = []
    for page in range(cache.shape[0]):
        started.append(pltpu.make_async_copy(cache.at[page], out.at[placement[page]], sem.at[page]))
        started[-1].start()
    for copy in started:
        copy.wait()


def pack(placement, cache, slots):
    return pl.pallas_call(
        pack_kernel,
        out_shape=jax.ShapeDtypeStruct((slots,) + cache.shape[1:], cache.dtype),
        in_specs=[spec(pltpu.SMEM), spec(pltpu.VMEM)],
        out_specs=spec(pl.ANY),
        scratch_shapes=[pltpu.SemaphoreType.DMA((cache.shape[0],))],
    )(placement, cache)


def unpack_kernel(chosen, incoming, out, sem):
    started = []
    for page in range(out.shape[0]):
        started.append(pltpu.make_async_copy(incoming.at[chosen[page]], out.at[page], sem.at[page]))
        started[-1].start()
    for copy in started:
        copy.wait()


def unpack(chosen, incoming):
    pages = chosen.shape[0]
    return pl.pallas_call(
        unpack_kernel,
        out_shape=jax.ShapeDtypeStruct((pages,) + incoming.shape[1:], incoming.dtype),
        in_specs=[spec(pltpu.SMEM), spec(pl.ANY)],
        out_specs=spec(pltpu.VMEM),
        scratch_shapes=[pltpu.SemaphoreType.DMA((pages,))],
    )(chosen, incoming)


def finish_kernel(mixing, attended, weight, depth, streams, out):
    layer_out = jnp.dot(attended[...], weight[...], preferred_element_type=jnp.float32)
    count = streams.shape[0]
    wide = [streams[source].astype(jnp.float32) for source in range(count)]
    for stream in range(count):
        carried = mixing[stream, 0] * wide[0]
        for source in range(1, count):
            carried = carried + mixing[stream, source] * wide[source]
        out[stream] = (carried + depth[:, stream : stream + 1] * layer_out).astype(out.dtype)


def finish(stream_mixing, attended, weight, depth, streams):
    count, tokens, width = streams.shape
    block = tokens // 4
    return pl.pallas_call(
        finish_kernel,
        grid=(tokens // block,),
        out_shape=jax.ShapeDtypeStruct(streams.shape, streams.dtype),
        in_specs=[
            spec(pltpu.SMEM),
            pl.BlockSpec((block, attended.shape[1]), lambda i: (i, 0)),
            pl.BlockSpec(weight.shape, lambda i: (0, 0)),
            pl.BlockSpec((block, count), lambda i: (i, 0)),
            pl.BlockSpec((count, block, width), lambda i: (0, i, 0)),
        ],
        out_specs=pl.BlockSpec((count, block, width), lambda i: (0, i, 0)),
        cost_estimate=pl.CostEstimate(flops=600_000_000, bytes_accessed=6_000_000, transcendentals=0),
    )(stream_mixing, attended, weight, depth, streams)


def gather_tokens(own):
    tokens, width = own.shape
    return pl.pallas_call(
        tokens_kernel,
        out_shape=jax.ShapeDtypeStruct((tokens, width * NY), own.dtype),
        in_specs=[spec(pltpu.VMEM)],
        out_specs=spec(pl.ANY),
        scratch_shapes=[
            pltpu.SemaphoreType.DMA((14,)),
            pltpu.SemaphoreType.DMA((14,)),
            pltpu.SemaphoreType.DMA((2,)),
        ],
        compiler_params=pltpu.CompilerParams(collective_id=1, has_side_effects=True),
        cost_estimate=pl.CostEstimate(flops=0, bytes_accessed=60_000_000, transcendentals=0),
    )(own)


def body(
    streams,
    doc_ids,
    doc_adapter,
    width_weights,
    stream_mixing,
    depth_static,
    depth_dir,
    qkv_weight,
    adapter_down,
    adapter_up,
    out_weight,
    page_slot,
):
    count_streams = streams.shape[0]
    tokens = streams.shape[1]
    page_count = page_slot.shape[0]
    width_local = qkv_weight.shape[2]
    rows_local = qkv_weight.shape[0]
    groups = lax.axis_size("req")
    target_dev = page_slot // page_count
    local_slot = page_slot % page_count
    capacity = 2 * max(1, page_count // (2 * groups))
    ordinal = jnp.arange(page_count)
    earlier = (target_dev[None, :] == target_dev[:, None]) & (ordinal[None, :] < ordinal[:, None])
    place = jnp.sum(earlier.astype(jnp.int32), axis=1)
    placement = target_dev * capacity + place
    lane = jnp.arange(128)[None, :]
    labels = jnp.where(
        lane == 0,
        target_dev[:, None],
        jnp.where(lane == 1, local_slot[:, None], jnp.where(lane == 2, place[:, None], 0)),
    ).astype(jnp.bfloat16)
    rows = jnp.concatenate([qkv_weight.reshape(rows_local, 3 * width_local), labels], axis=1)
    gathered, rows_all, out_all, down_all = gather_all(
        mix_in(width_weights, streams), rows, out_weight, adapter_down.transpose(0, 2, 1)
    )
    rows_all = rows_all.reshape(groups * rows_local, -1)
    out_all = out_all.reshape(groups * rows_local, width_local)
    qkv_all = rows_all[:, : 3 * width_local]
    label_all = rows_all[:, 3 * width_local : 3 * width_local + 3].astype(jnp.int32)
    came = label_all[:, 0] == lax.axis_index("req")
    came_row = (jnp.arange(groups * page_count) // page_count) * capacity + label_all[:, 2]
    chosen = jnp.sum(
        jnp.where(came[None, :] & (label_all[:, 1][None, :] == ordinal[:, None]), came_row[None, :], 0), axis=1
    )

    widened = gathered.astype(jnp.float32)
    normed = (
        widened * lax.rsqrt(jnp.mean(widened * widened, axis=-1, keepdims=True) + EPSILON)
    ).astype(jnp.bfloat16)
    segment = doc_ids[0]
    doc_table = doc_adapter[0, :, 0]
    token_adapter = jnp.sum(
        jnp.where(
            segment[:, None] == jnp.arange(doc_table.shape[0])[None, :], doc_table[None, :], 0
        ),
        axis=1,
    )
    adapters_total = adapter_up.shape[0]
    lanes = jnp.arange(adapters_total * R)[None, :]
    own_lane = token_adapter[:, None] == lanes // R
    every_rank = lax.dot_general(
        normed,
        down_all.reshape(adapters_total * R, -1),
        (((1,), (1,)), ((), ())),
        preferred_element_type=jnp.float32,
    )
    spread = jnp.where(own_lane, every_rank, 0.0).astype(jnp.bfloat16)
    lowrank = jnp.dot(
        spread, adapter_up.reshape(adapters_total * R, -1), preferred_element_type=jnp.float32
    )
    base = jnp.dot(normed, qkv_all, preferred_element_type=jnp.float32)
    heads_local = width_local // HD
    projected = (base + lowrank).astype(jnp.bfloat16)
    positions = jnp.arange(tokens)
    allowed = (segment[:, None] == segment[None, :]) & (positions[None, :] <= positions[:, None])
    parts = []
    for head in range(heads_local):
        query, key, value = (
            projected[:, part * width_local + head * HD : part * width_local + (head + 1) * HD]
            for part in range(3)
        )
        scores = lax.dot_general(
            query, key, (((1,), (1,)), ((), ())), preferred_element_type=jnp.float32
        ) / math.sqrt(HD)
        scores = jnp.where(allowed, scores, -1e30)
        highest = jnp.max(scores, axis=-1, keepdims=True)
        weights = jnp.exp(scores - highest)
        weights = (weights / jnp.sum(weights, axis=-1, keepdims=True)).astype(jnp.bfloat16)
        parts.append(jnp.dot(weights, value, preferred_element_type=jnp.float32).astype(jnp.bfloat16))
    attended = gather_tokens(jnp.concatenate(parts, axis=1))
    depth = depth_static[None, :] + jnp.tanh(
        jnp.dot(normed, depth_dir, preferred_element_type=jnp.float32)
    )
    new_streams = finish(stream_mixing, attended, out_all, depth, streams)

    cache = projected[:, width_local:].reshape(page_count, PAGE, 2 * width_local)
    outgoing = pack(placement, cache, groups * capacity)
    incoming = lax.all_to_all(outgoing, "req", split_axis=0, concat_axis=0, tiled=True)
    kv_pool = unpack(chosen, incoming).reshape(page_count, PAGE, 2, width_local)
    return (new_streams, kv_pool)


def solution(mesh):
    in_specs = (
        P(None, "req", "wt"),
        P("req", None),
        P("req", None, None),
        P(),
        P(),
        P(),
        P(),
        P("req", None, "wt"),
        P("wt", None, None),
        P(None, None, None, "wt"),
        P("req", "wt"),
        P("req"),
    )
    out_specs = (P(None, "req", "wt"), P("req", None, None, "wt"))
    return jax.shard_map(body, mesh=mesh, in_specs=in_specs, out_specs=out_specs, check_vma=False)
```

```python
import functools
import math

import jax
import jax.numpy as jnp
from jax import lax
from jax.experimental import pallas as pl
from jax.experimental.pallas import tpu as pltpu
from jax.sharding import PartitionSpec as P

HD = 128
R = 16
PAGE = 16
NX, NZ, NC, NY = 4, 8, 2, 8

EPSILON = 1e-05
MESH = pl.DeviceIdType.MESH


class Copies:
    def __init__(self, send_sem, recv_sem):
        self.send_sem, self.recv_sem = send_sem, recv_sem
        self.count = 0
        self.started = []

    def start(self, src, dst, req, wt):
        index = self.count
        self.count += 1
        copy = pltpu.make_async_remote_copy(
            src_ref=src,
            dst_ref=dst,
            send_sem=self.send_sem.at[index],
            recv_sem=self.recv_sem.at[index],
            device_id=(req, wt),
            device_id_type=MESH,
        )
        copy.start()
        self.started.append(copy)
        return copy

    def finish(self):
        for copy in self.started:
            copy.wait_send()


def position():
    req = lax.axis_index("req")
    wt = lax.axis_index("wt")
    core = lax.rem(req, NC)
    z = lax.rem(req // NC, NZ)
    x = req // (NC * NZ)
    return req, wt, x, z, core


def turn(value, shift, size):
    return lax.rem(value + (shift + size), size)


def meet(partners):
    barrier = pltpu.get_barrier_semaphore()
    for req, wt in partners:
        pl.semaphore_signal(barrier, inc=1, device_id=(req, wt), device_id_type=MESH)
    pl.semaphore_wait(barrier, len(partners))


def columns(ref, half, origin):
    rows = ref.shape[0] // 2
    width = ref.shape[1] // NY
    return ref.at[pl.ds(half * rows, rows), pl.ds(pl.multiple_of(origin * width, width), width)]


def token_hop(copies, held, own, out, req, wt, half, direction, step):
    if step == 3 and half != (0 if direction == 1 else 1):
        return
    key = (half, direction)
    if step > 0:
        held[key].wait_recv()
    origin = turn(wt, -direction * step, NY)
    rows = out.shape[0] // 2
    src = own.at[pl.ds(half * rows, rows)] if step == 0 else columns(out, half, origin)
    held[key] = copies.start(src, columns(out, half, origin), req, turn(wt, direction, NY))


def gather_kernel(
    mixed, rows, out_rows, down, mixed_all, rows_all, out_all, down_all, send_sem, recv_sem, local_sem
):
    req, wt, x, z, core = position()
    partner = req + 1 - 2 * core

    def at(x_at, z_at):
        return (x_at * NZ + z_at) * NC + core

    def near_x(shift):
        return at(turn(x, shift, NX), z)

    def near_z(shift):
        return at(x, turn(z, shift, NZ))

    meet(
        [(partner, wt)]
        + [(req, turn(wt, shift, NY)) for shift in range(1, NY)]
        + [(near_z(shift), wt) for shift in range(1, NZ)]
        + [(near_x(shift), wt) for shift in range(1, NX)]
    )
    copies = Copies(send_sem, recv_sem)
    held_tokens, held_rows = {}, {}
    slice_width = down.shape[2] // NX
    both = (1, -1)

    def down_lanes(x_at):
        return pl.ds(pl.multiple_of(x_at * slice_width, slice_width), slice_width)

    def rows_hop(unit, step):
        for direction in both:
            if step == 3 and unit % 2 != (0 if direction == 1 else 1):
                continue
            key = (unit, direction)
            if step > 0:
                held_rows[key].wait_recv()
            block = rows_all.at[turn(x, -unit, NX), turn(z, -direction * step, NZ), core]
            src = rows if (step == 0 and unit == 0) else block
            held_rows[key] = copies.start(src, block, near_z(direction), wt)

    def token_step(half, step):
        for direction in both:
            token_hop(copies, held_tokens, mixed, mixed_all, req, wt, half, direction, step)

    def share(z_shift):
        block = rows_all.at[:, turn(z, z_shift, NZ), core]
        return copies.start(block, block, partner, wt)

    own_rows = rows_all.at[x, z, core]
    own_out = out_all.at[x, z, core]
    own_down = down_all.at[wt, core, :, down_lanes(x)]
    small = []
    for shift in (1, 7, 2, 6, 3, 5, 4):
        small.append(copies.start(out_rows, own_out, near_z(shift), wt))
        small.append(copies.start(down.at[core, :, down_lanes(x)], own_down, req, turn(wt, shift, NY)))
    along_x = {shift: copies.start(rows, own_rows, near_x(shift), wt) for shift in (1, 3, 2)}
    token_step(0, 0)
    rows_hop(0, 0)
    token_step(1, 0)
    half = mixed.shape[0] // 2
    locals_ = [
        pltpu.make_async_copy(rows, own_rows, local_sem.at[0]),
        pltpu.make_async_copy(mixed.at[pl.ds(0, half)], columns(mixed_all, 0, wt), local_sem.at[1]),
        pltpu.make_async_copy(mixed.at[pl.ds(half, half)], columns(mixed_all, 1, wt), local_sem.at[2]),
        pltpu.make_async_copy(down.at[core, :, down_lanes(x)], own_down, local_sem.at[3]),
        pltpu.make_async_copy(out_rows, own_out, local_sem.at[4]),
    ]
    for copy in locals_:
        copy.start()
    for shift in (1, 3, 2):
        along_x[shift].wait_recv()
        rows_hop(shift, 0)
    for copy in locals_:
        copy.wait()
    shared = [share(0)]
    rows_hop(0, 1)
    for copy in small:
        copy.wait_recv()
    down_block, out_block = down_all.at[:, core, :, down_lanes(x)], out_all.at[x, :, core]
    small = []
    for shift in (1, 3, 2):
        for block in (down_block, out_block):
            small.append(copies.start(block, block, near_x(shift), wt))
    for unit in (1, 3, 2):
        rows_hop(unit, 1)
    shared += [share(-1), share(1)]
    token_step(0, 1)
    rows_hop(0, 2)
    rows_hop(1, 2)
    token_step(1, 1)
    rows_hop(3, 2)
    rows_hop(2, 2)
    shared += [share(-2), share(2)]
    rows_hop(0, 3)
    token_step(0, 2)
    rows_hop(1, 3)
    rows_hop(3, 3)
    token_step(1, 2)
    rows_hop(2, 3)
    for copy in small:
        copy.wait_recv()
    for block in (down_all.at[:, core], out_all.at[:, :, core]):
        shared.append(copies.start(block, block, partner, wt))
    token_step(0, 3)
    for key in ((1, 1), (3, 1), (0, -1), (2, -1)):
        held_rows[key].wait_recv()
    shared += [share(-3), share(3)]
    for key in ((0, 1), (2, 1), (1, -1), (3, -1)):
        held_rows[key].wait_recv()
    shared.append(share(4))
    token_step(1, 3)
    for half in (0, 1):
        for direction in both:
            held_tokens[(half, direction)].wait_recv()
    for copy in shared:
        copy.wait_recv()
    copies.finish()


def tokens_kernel(own, out, send_sem, recv_sem, local_sem):
    req, wt, _, _, _ = position()
    meet([(req, turn(wt, 1, NY)), (req, turn(wt, -1, NY))])
    copies = Copies(send_sem, recv_sem)
    held = {}
    rows = own.shape[0] // 2
    locals_ = []
    for step in range(4):
        for half in (0, 1):
            for direction in (1, -1):
                token_hop(copies, held, own, out, req, wt, half, direction, step)
            if step == 0:
                locals_.append(
                    pltpu.make_async_copy(own.at[pl.ds(half * rows, rows)], columns(out, half, wt), local_sem.at[half])
                )
                locals_[-1].start()
    for half in (0, 1):
        for direction in (1, -1):
            held[(half, direction)].wait_recv()
    for copy in locals_:
        copy.wait()
    copies.finish()


def spec(space):
    return pl.BlockSpec(memory_space=space)


def gather_all(mixed, rows, out_rows, down):
    tokens, width = mixed.shape
    count = 3 + 28 + 8 + 14 + 2 * (7 + 3 + 1)
    return pl.pallas_call(
        gather_kernel,
        out_shape=[
            jax.ShapeDtypeStruct((tokens, width * NY), mixed.dtype),
            jax.ShapeDtypeStruct((NX, NZ, NC) + rows.shape, rows.dtype),
            jax.ShapeDtypeStruct((NX, NZ, NC) + out_rows.shape, out_rows.dtype),
            jax.ShapeDtypeStruct((NY,) + down.shape, down.dtype),
        ],
        in_specs=[spec(pltpu.VMEM)] * 4,
        out_specs=[spec(pl.ANY)] * 4,
        scratch_shapes=[
            pltpu.SemaphoreType.DMA((count,)),
            pltpu.SemaphoreType.DMA((count,)),
            pltpu.SemaphoreType.DMA((5,)),
        ],
        compiler_params=pltpu.CompilerParams(collective_id=0, has_side_effects=True),
    )(mixed, rows, out_rows, down)


def mixed_kernel(weights, streams, out):
    total = weights[0] * streams[0].astype(jnp.float32)
    for stream in range(1, streams.shape[0]):
        total = total + weights[stream] * streams[stream].astype(jnp.float32)
    out[...] = total.astype(out.dtype)


def mix_in(width_weights, streams):
    count, tokens, width = streams.shape
    block = tokens // 2
    return pl.pallas_call(
        mixed_kernel,
        grid=(tokens // block,),
        out_shape=jax.ShapeDtypeStruct((tokens, width), streams.dtype),
        in_specs=[spec(pltpu.SMEM), pl.BlockSpec((count, block, width), lambda i: (0, i, 0))],
        out_specs=pl.BlockSpec((block, width), lambda i: (i, 0)),
    )(width_weights, streams)


def pack_kernel(placement, cache, out, sem):
    started = []
    for page in range(cache.shape[0]):
        started.append(pltpu.make_async_copy(cache.at[page], out.at[placement[page]], sem.at[page]))
        started[-1].start()
    for copy in started:
        copy.wait()


def pack(placement, cache, slots):
    return pl.pallas_call(
        pack_kernel,
        out_shape=jax.ShapeDtypeStruct((slots,) + cache.shape[1:], cache.dtype),
        in_specs=[spec(pltpu.SMEM), spec(pltpu.VMEM)],
        out_specs=spec(pl.ANY),
        scratch_shapes=[pltpu.SemaphoreType.DMA((cache.shape[0],))],
    )(placement, cache)


def unpack_kernel(chosen, incoming, out):
    for page in range(out.shape[0]):
        out[page] = incoming[chosen[page]]


def unpack(chosen, incoming):
    pages = chosen.shape[0]
    return pl.pallas_call(
        unpack_kernel,
        out_shape=jax.ShapeDtypeStruct((pages,) + incoming.shape[1:], incoming.dtype),
        in_specs=[spec(pltpu.SMEM), spec(pltpu.VMEM)],
        out_specs=spec(pltpu.VMEM),
    )(chosen, incoming)


def finish_kernel(mixing, attended, weight, depth, streams, out):
    layer_out = jnp.dot(attended[...], weight[...], preferred_element_type=jnp.float32)
    count = streams.shape[0]
    wide = [streams[source].astype(jnp.float32) for source in range(count)]
    for stream in range(count):
        carried = mixing[stream, 0] * wide[0]
        for source in range(1, count):
            carried = carried + mixing[stream, source] * wide[source]
        out[stream] = (carried + depth[:, stream : stream + 1] * layer_out).astype(out.dtype)


def finish(stream_mixing, attended, weight, depth, streams):
    count, tokens, width = streams.shape
    block = tokens // 4
    return pl.pallas_call(
        finish_kernel,
        grid=(tokens // block,),
        out_shape=jax.ShapeDtypeStruct(streams.shape, streams.dtype),
        in_specs=[
            spec(pltpu.SMEM),
            pl.BlockSpec((block, attended.shape[1]), lambda i: (i, 0)),
            pl.BlockSpec(weight.shape, lambda i: (0, 0)),
            pl.BlockSpec((block, count), lambda i: (i, 0)),
            pl.BlockSpec((count, block, width), lambda i: (0, i, 0)),
        ],
        out_specs=pl.BlockSpec((count, block, width), lambda i: (0, i, 0)),
        cost_estimate=pl.CostEstimate(flops=600_000_000, bytes_accessed=6_000_000, transcendentals=0),
    )(stream_mixing, attended, weight, depth, streams)


def gather_tokens(own):
    tokens, width = own.shape
    return pl.pallas_call(
        tokens_kernel,
        out_shape=jax.ShapeDtypeStruct((tokens, width * NY), own.dtype),
        in_specs=[spec(pltpu.VMEM)],
        out_specs=spec(pl.ANY),
        scratch_shapes=[
            pltpu.SemaphoreType.DMA((14,)),
            pltpu.SemaphoreType.DMA((14,)),
            pltpu.SemaphoreType.DMA((2,)),
        ],
        compiler_params=pltpu.CompilerParams(collective_id=1, has_side_effects=True),
        cost_estimate=pl.CostEstimate(flops=0, bytes_accessed=60_000_000, transcendentals=0),
    )(own)


def body(
    streams,
    doc_ids,
    doc_adapter,
    width_weights,
    stream_mixing,
    depth_static,
    depth_dir,
    qkv_weight,
    adapter_down,
    adapter_up,
    out_weight,
    page_slot,
):
    count_streams = streams.shape[0]
    tokens = streams.shape[1]
    page_count = page_slot.shape[0]
    width_local = qkv_weight.shape[2]
    rows_local = qkv_weight.shape[0]
    groups = lax.axis_size("req")
    target_dev = page_slot // page_count
    local_slot = page_slot % page_count
    capacity = 2 * max(1, page_count // (2 * groups))
    ordinal = jnp.arange(page_count)
    earlier = (target_dev[None, :] == target_dev[:, None]) & (ordinal[None, :] < ordinal[:, None])
    place = jnp.sum(earlier.astype(jnp.int32), axis=1)
    placement = target_dev * capacity + place
    lane = jnp.arange(128)[None, :]
    labels = jnp.where(
        lane == 0,
        target_dev[:, None],
        jnp.where(lane == 1, local_slot[:, None], jnp.where(lane == 2, place[:, None], 0)),
    ).astype(jnp.bfloat16)
    rows = jnp.concatenate([qkv_weight.reshape(rows_local, 3 * width_local), labels], axis=1)
    gathered, rows_all, out_all, down_all = gather_all(
        mix_in(width_weights, streams), rows, out_weight, adapter_down.transpose(0, 2, 1)
    )
    rows_all = rows_all.reshape(groups * rows_local, -1)
    out_all = out_all.reshape(groups * rows_local, width_local)
    qkv_all = rows_all[:, : 3 * width_local]
    label_all = rows_all[:, 3 * width_local : 3 * width_local + 3].astype(jnp.int32)
    came = label_all[:, 0] == lax.axis_index("req")
    came_row = (jnp.arange(groups * page_count) // page_count) * capacity + label_all[:, 2]
    chosen = jnp.sum(
        jnp.where(came[None, :] & (label_all[:, 1][None, :] == ordinal[:, None]), came_row[None, :], 0), axis=1
    )

    widened = gathered.astype(jnp.float32)
    normed = (
        widened * lax.rsqrt(jnp.mean(widened * widened, axis=-1, keepdims=True) + EPSILON)
    ).astype(jnp.bfloat16)
    segment = doc_ids[0]
    doc_table = doc_adapter[0, :, 0]
    token_adapter = jnp.sum(
        jnp.where(
            segment[:, None] == jnp.arange(doc_table.shape[0])[None, :], doc_table[None, :], 0
        ),
        axis=1,
    )
    adapters_total = adapter_up.shape[0]
    lanes = jnp.arange(adapters_total * R)[None, :]
    own_lane = token_adapter[:, None] == lanes // R
    every_rank = lax.dot_general(
        normed,
        down_all.reshape(adapters_total * R, -1),
        (((1,), (1,)), ((), ())),
        preferred_element_type=jnp.float32,
    )
    spread = jnp.where(own_lane, every_rank, 0.0).astype(jnp.bfloat16)
    up = adapter_up.reshape(adapters_total * R, -1)

    def project(start, stop):
        base = jnp.dot(normed, qkv_all[:, start:stop], preferred_element_type=jnp.float32)
        lowrank = jnp.dot(spread, up[:, start:stop], preferred_element_type=jnp.float32)
        return (base + lowrank).astype(jnp.bfloat16)

    heads_local = width_local // HD
    cache = project(width_local, 3 * width_local)
    queries = project(0, width_local)
    positions = jnp.arange(tokens)
    allowed = (segment[:, None] == segment[None, :]) & (positions[None, :] <= positions[:, None])
    parts = []
    for head in range(heads_local):
        at = head * HD
        query = queries[:, at : at + HD]
        key = cache[:, at : at + HD]
        value = cache[:, width_local + at : width_local + at + HD]
        scores = lax.dot_general(
            query, key, (((1,), (1,)), ((), ())), preferred_element_type=jnp.float32
        ) / math.sqrt(HD)
        scores = jnp.where(allowed, scores, -1e30)
        highest = jnp.max(scores, axis=-1, keepdims=True)
        weights = jnp.exp(scores - highest)
        weights = (weights / jnp.sum(weights, axis=-1, keepdims=True)).astype(jnp.bfloat16)
        parts.append(jnp.dot(weights, value, preferred_element_type=jnp.float32).astype(jnp.bfloat16))
    attended = gather_tokens(jnp.concatenate(parts, axis=1))
    depth = depth_static[None, :] + jnp.tanh(
        jnp.dot(normed, depth_dir, preferred_element_type=jnp.float32)
    )
    new_streams = finish(stream_mixing, attended, out_all, depth, streams)

    outgoing = pack(placement, cache.reshape(page_count, PAGE, 2 * width_local), groups * capacity)
    incoming = lax.all_to_all(outgoing, "req", split_axis=0, concat_axis=0, tiled=True)
    kv_pool = unpack(chosen, incoming).reshape(page_count, PAGE, 2, width_local)
    return (new_streams, kv_pool)


def solution(mesh):
    in_specs = (
        P(None, "req", "wt"),
        P("req", None),
        P("req", None, None),
        P(),
        P(),
        P(),
        P(),
        P("req", None, "wt"),
        P("wt", None, None),
        P(None, None, None, "wt"),
        P("req", "wt"),
        P("req"),
    )
    out_specs = (P(None, "req", "wt"), P("req", None, None, "wt"))
    return jax.shard_map(body, mesh=mesh, in_specs=in_specs, out_specs=out_specs, check_vma=False)
```

```python
import functools
import math

import jax
import jax.numpy as jnp
from jax import lax
from jax.experimental import pallas as pl
from jax.experimental.pallas import tpu as pltpu
from jax.sharding import PartitionSpec as P

HD = 128
R = 16
PAGE = 16
NX, NZ, NC, NY = 4, 8, 2, 8

EPSILON = 1e-05
MESH = pl.DeviceIdType.MESH


class Copies:
    def __init__(self, send_sem, recv_sem):
        self.send_sem, self.recv_sem = send_sem, recv_sem
        self.count = 0
        self.started = []

    def start(self, src, dst, req, wt):
        index = self.count
        self.count += 1
        copy = pltpu.make_async_remote_copy(
            src_ref=src,
            dst_ref=dst,
            send_sem=self.send_sem.at[index],
            recv_sem=self.recv_sem.at[index],
            device_id=(req, wt),
            device_id_type=MESH,
        )
        copy.start()
        self.started.append(copy)
        return copy

    def finish(self):
        for copy in self.started:
            copy.wait_send()


def position():
    req = lax.axis_index("req")
    wt = lax.axis_index("wt")
    core = lax.rem(req, NC)
    z = lax.rem(req // NC, NZ)
    x = req // (NC * NZ)
    return req, wt, x, z, core


def turn(value, shift, size):
    return lax.rem(value + (shift + size), size)


def meet(partners):
    barrier = pltpu.get_barrier_semaphore()
    for req, wt in partners:
        pl.semaphore_signal(barrier, inc=1, device_id=(req, wt), device_id_type=MESH)
    pl.semaphore_wait(barrier, len(partners))


def columns(ref, half, origin):
    rows = ref.shape[0] // 2
    width = ref.shape[1] // NY
    return ref.at[pl.ds(half * rows, rows), pl.ds(pl.multiple_of(origin * width, width), width)]


def token_hop(copies, held, own, out, req, wt, half, direction, step):
    if step == 3 and half != (0 if direction == 1 else 1):
        return
    key = (half, direction)
    if step > 0:
        held[key].wait_recv()
    origin = turn(wt, -direction * step, NY)
    rows = out.shape[0] // 2
    src = own.at[pl.ds(half * rows, rows)] if step == 0 else columns(out, half, origin)
    held[key] = copies.start(src, columns(out, half, origin), req, turn(wt, direction, NY))


def gather_kernel(
    mixed, rows, out_rows, down, mixed_all, rows_all, out_all, down_all, send_sem, recv_sem, local_sem
):
    req, wt, x, z, core = position()
    partner = req + 1 - 2 * core

    def at(x_at, z_at):
        return (x_at * NZ + z_at) * NC + core

    def near_x(shift):
        return at(turn(x, shift, NX), z)

    def near_z(shift):
        return at(x, turn(z, shift, NZ))

    meet(
        [(partner, wt)]
        + [(req, turn(wt, shift, NY)) for shift in range(1, NY)]
        + [(near_z(shift), wt) for shift in range(1, NZ)]
        + [(near_x(shift), wt) for shift in range(1, NX)]
    )
    copies = Copies(send_sem, recv_sem)
    held_tokens, held_rows = {}, {}
    slice_width = down.shape[2] // NX
    both = (1, -1)

    def down_lanes(x_at):
        return pl.ds(pl.multiple_of(x_at * slice_width, slice_width), slice_width)

    def rows_hop(unit, step):
        for direction in both:
            if step == 3 and unit % 2 != (0 if direction == 1 else 1):
                continue
            key = (unit, direction)
            if step > 0:
                held_rows[key].wait_recv()
            block = rows_all.at[turn(x, -unit, NX), turn(z, -direction * step, NZ), core]
            src = rows if (step == 0 and unit == 0) else block
            held_rows[key] = copies.start(src, block, near_z(direction), wt)

    def token_step(half, step):
        for direction in both:
            token_hop(copies, held_tokens, mixed, mixed_all, req, wt, half, direction, step)

    def share(z_shift):
        block = rows_all.at[:, turn(z, z_shift, NZ), core]
        return copies.start(block, block, partner, wt)

    own_rows = rows_all.at[x, z, core]
    own_out = out_all.at[x, z, core]
    own_down = down_all.at[wt, core, :, down_lanes(x)]
    small = []
    for shift in (1, 7, 2, 6, 3, 5, 4):
        small.append(copies.start(out_rows, own_out, near_z(shift), wt))
        small.append(copies.start(down.at[core, :, down_lanes(x)], own_down, req, turn(wt, shift, NY)))
    along_x = {shift: copies.start(rows, own_rows, near_x(shift), wt) for shift in (1, 3, 2)}
    token_step(0, 0)
    rows_hop(0, 0)
    token_step(1, 0)
    half = mixed.shape[0] // 2
    locals_ = [
        pltpu.make_async_copy(rows, own_rows, local_sem.at[0]),
        pltpu.make_async_copy(mixed.at[pl.ds(0, half)], columns(mixed_all, 0, wt), local_sem.at[1]),
        pltpu.make_async_copy(mixed.at[pl.ds(half, half)], columns(mixed_all, 1, wt), local_sem.at[2]),
        pltpu.make_async_copy(down.at[core, :, down_lanes(x)], own_down, local_sem.at[3]),
        pltpu.make_async_copy(out_rows, own_out, local_sem.at[4]),
    ]
    for copy in locals_:
        copy.start()
    for shift in (1, 3, 2):
        along_x[shift].wait_recv()
        rows_hop(shift, 0)
    for copy in locals_:
        copy.wait()
    shared = [share(0)]
    rows_hop(0, 1)
    for copy in small:
        copy.wait_recv()
    down_block, out_block = down_all.at[:, core, :, down_lanes(x)], out_all.at[x, :, core]
    small = []
    for shift in (1, 3, 2):
        for block in (down_block, out_block):
            small.append(copies.start(block, block, near_x(shift), wt))
    for unit in (1, 3, 2):
        rows_hop(unit, 1)
    shared += [share(-1), share(1)]
    token_step(0, 1)
    rows_hop(0, 2)
    rows_hop(1, 2)
    token_step(1, 1)
    rows_hop(3, 2)
    rows_hop(2, 2)
    shared += [share(-2), share(2)]
    rows_hop(0, 3)
    token_step(0, 2)
    rows_hop(1, 3)
    rows_hop(3, 3)
    token_step(1, 2)
    rows_hop(2, 3)
    for copy in small:
        copy.wait_recv()
    for block in (down_all.at[:, core], out_all.at[:, :, core]):
        shared.append(copies.start(block, block, partner, wt))
    token_step(0, 3)
    for key in ((1, 1), (3, 1), (0, -1), (2, -1)):
        held_rows[key].wait_recv()
    shared += [share(-3), share(3)]
    for key in ((0, 1), (2, 1), (1, -1), (3, -1)):
        held_rows[key].wait_recv()
    shared.append(share(4))
    token_step(1, 3)
    for half in (0, 1):
        for direction in both:
            held_tokens[(half, direction)].wait_recv()
    for copy in shared:
        copy.wait_recv()
    copies.finish()


def tokens_kernel(own, out, send_sem, recv_sem, local_sem):
    req, wt, _, _, _ = position()
    meet([(req, turn(wt, 1, NY)), (req, turn(wt, -1, NY))])
    copies = Copies(send_sem, recv_sem)
    held = {}
    rows = own.shape[0] // 2
    locals_ = []
    for step in range(4):
        for half in (0, 1):
            for direction in (1, -1):
                token_hop(copies, held, own, out, req, wt, half, direction, step)
            if step == 0:
                locals_.append(
                    pltpu.make_async_copy(own.at[pl.ds(half * rows, rows)], columns(out, half, wt), local_sem.at[half])
                )
                locals_[-1].start()
    for half in (0, 1):
        for direction in (1, -1):
            held[(half, direction)].wait_recv()
    for copy in locals_:
        copy.wait()
    copies.finish()


def spec(space):
    return pl.BlockSpec(memory_space=space)


def gather_all(mixed, rows, out_rows, down):
    tokens, width = mixed.shape
    count = 3 + 28 + 8 + 14 + 2 * (7 + 3 + 1)
    return pl.pallas_call(
        gather_kernel,
        out_shape=[
            jax.ShapeDtypeStruct((tokens, width * NY), mixed.dtype),
            jax.ShapeDtypeStruct((NX, NZ, NC) + rows.shape, rows.dtype),
            jax.ShapeDtypeStruct((NX, NZ, NC) + out_rows.shape, out_rows.dtype),
            jax.ShapeDtypeStruct((NY,) + down.shape, down.dtype),
        ],
        in_specs=[spec(pltpu.VMEM)] * 4,
        out_specs=[spec(pl.ANY)] * 4,
        scratch_shapes=[
            pltpu.SemaphoreType.DMA((count,)),
            pltpu.SemaphoreType.DMA((count,)),
            pltpu.SemaphoreType.DMA((5,)),
        ],
        compiler_params=pltpu.CompilerParams(collective_id=0, has_side_effects=True),
    )(mixed, rows, out_rows, down)


def mixed_kernel(weights, streams, qkv, labels, out, rows):
    total = weights[0] * streams[0].astype(jnp.float32)
    for stream in range(1, streams.shape[0]):
        total = total + weights[stream] * streams[stream].astype(jnp.float32)
    out[...] = total.astype(out.dtype)

    @pl.when(pl.program_id(0) == 0)
    def _():
        width = qkv.shape[2]
        block = qkv[...]
        for part in range(3):
            rows[:, part * width : (part + 1) * width] = block[:, part, :]
        rows[:, 3 * width :] = labels[...]


def mix_in(width_weights, streams, qkv, labels):
    count, tokens, width = streams.shape
    block = tokens // 2
    row_shape = (qkv.shape[0], 3 * qkv.shape[2] + labels.shape[1])
    return pl.pallas_call(
        mixed_kernel,
        grid=(tokens // block,),
        out_shape=[
            jax.ShapeDtypeStruct((tokens, width), streams.dtype),
            jax.ShapeDtypeStruct(row_shape, qkv.dtype),
        ],
        in_specs=[
            spec(pltpu.SMEM),
            pl.BlockSpec((count, block, width), lambda i: (0, i, 0)),
            pl.BlockSpec(qkv.shape, lambda i: (0, 0, 0)),
            pl.BlockSpec(labels.shape, lambda i: (0, 0)),
        ],
        out_specs=[
            pl.BlockSpec((block, width), lambda i: (i, 0)),
            pl.BlockSpec(row_shape, lambda i: (0, 0)),
        ],
    )(width_weights, streams, qkv, labels)


def pack_kernel(placement, cache, out, sem):
    started = []
    for page in range(cache.shape[0]):
        started.append(pltpu.make_async_copy(cache.at[page], out.at[placement[page]], sem.at[page]))
        started[-1].start()
    for copy in started:
        copy.wait()


def pack(placement, cache, slots):
    return pl.pallas_call(
        pack_kernel,
        out_shape=jax.ShapeDtypeStruct((slots,) + cache.shape[1:], cache.dtype),
        in_specs=[spec(pltpu.SMEM), spec(pltpu.VMEM)],
        out_specs=spec(pl.ANY),
        scratch_shapes=[pltpu.SemaphoreType.DMA((cache.shape[0],))],
    )(placement, cache)


def unpack_kernel(chosen, incoming, out):
    for page in range(out.shape[0]):
        out[page] = incoming[chosen[page]]


def unpack(chosen, incoming):
    pages = chosen.shape[0]
    return pl.pallas_call(
        unpack_kernel,
        out_shape=jax.ShapeDtypeStruct((pages,) + incoming.shape[1:], incoming.dtype),
        in_specs=[spec(pltpu.SMEM), spec(pltpu.VMEM)],
        out_specs=spec(pltpu.VMEM),
    )(chosen, incoming)


def finish_kernel(mixing, attended, weight, depth, streams, out):
    layer_out = jnp.dot(attended[...], weight[...], preferred_element_type=jnp.float32)
    count = streams.shape[0]
    wide = [streams[source].astype(jnp.float32) for source in range(count)]
    for stream in range(count):
        carried = mixing[stream, 0] * wide[0]
        for source in range(1, count):
            carried = carried + mixing[stream, source] * wide[source]
        out[stream] = (carried + depth[:, stream : stream + 1] * layer_out).astype(out.dtype)


def finish(stream_mixing, attended, weight, depth, streams):
    count, tokens, width = streams.shape
    block = tokens // 4
    return pl.pallas_call(
        finish_kernel,
        grid=(tokens // block,),
        out_shape=jax.ShapeDtypeStruct(streams.shape, streams.dtype),
        in_specs=[
            spec(pltpu.SMEM),
            pl.BlockSpec((block, attended.shape[1]), lambda i: (i, 0)),
            pl.BlockSpec(weight.shape, lambda i: (0, 0)),
            pl.BlockSpec((block, count), lambda i: (i, 0)),
            pl.BlockSpec((count, block, width), lambda i: (0, i, 0)),
        ],
        out_specs=pl.BlockSpec((count, block, width), lambda i: (0, i, 0)),
        cost_estimate=pl.CostEstimate(flops=600_000_000, bytes_accessed=6_000_000, transcendentals=0),
    )(stream_mixing, attended, weight, depth, streams)


def gather_tokens(own):
    tokens, width = own.shape
    return pl.pallas_call(
        tokens_kernel,
        out_shape=jax.ShapeDtypeStruct((tokens, width * NY), own.dtype),
        in_specs=[spec(pltpu.VMEM)],
        out_specs=spec(pl.ANY),
        scratch_shapes=[
            pltpu.SemaphoreType.DMA((14,)),
            pltpu.SemaphoreType.DMA((14,)),
            pltpu.SemaphoreType.DMA((2,)),
        ],
        compiler_params=pltpu.CompilerParams(
            collective_id=1, has_side_effects=True, vmem_limit_bytes=66_000_000
        ),
        cost_estimate=pl.CostEstimate(flops=0, bytes_accessed=60_000_000, transcendentals=0),
    )(own)


def body(
    streams,
    doc_ids,
    doc_adapter,
    width_weights,
    stream_mixing,
    depth_static,
    depth_dir,
    qkv_weight,
    adapter_down,
    adapter_up,
    out_weight,
    page_slot,
):
    count_streams = streams.shape[0]
    tokens = streams.shape[1]
    page_count = page_slot.shape[0]
    width_local = qkv_weight.shape[2]
    rows_local = qkv_weight.shape[0]
    groups = lax.axis_size("req")
    target_dev = page_slot // page_count
    local_slot = page_slot % page_count
    capacity = 2 * max(1, page_count // (2 * groups))
    ordinal = jnp.arange(page_count)
    earlier = (target_dev[None, :] == target_dev[:, None]) & (ordinal[None, :] < ordinal[:, None])
    place = jnp.sum(earlier.astype(jnp.int32), axis=1)
    placement = target_dev * capacity + place
    lane = jnp.arange(128)[None, :]
    labels = jnp.where(
        lane == 0,
        target_dev[:, None],
        jnp.where(lane == 1, local_slot[:, None], jnp.where(lane == 2, place[:, None], 0)),
    ).astype(jnp.bfloat16)
    mixed_local, rows = mix_in(width_weights, streams, qkv_weight, labels)
    gathered, rows_all, out_all, down_all = gather_all(
        mixed_local, rows, out_weight, adapter_down.transpose(0, 2, 1)
    )
    rows_all = rows_all.reshape(groups * rows_local, -1)
    out_all = out_all.reshape(groups * rows_local, width_local)
    qkv_all = rows_all[:, : 3 * width_local]
    label_all = rows_all[:, 3 * width_local : 3 * width_local + 3].astype(jnp.int32)
    came = label_all[:, 0] == lax.axis_index("req")
    came_row = (jnp.arange(groups * page_count) // page_count) * capacity + label_all[:, 2]
    chosen = jnp.sum(
        jnp.where(came[None, :] & (label_all[:, 1][None, :] == ordinal[:, None]), came_row[None, :], 0), axis=1
    )

    widened = gathered.astype(jnp.float32)
    normed = (
        widened * lax.rsqrt(jnp.mean(widened * widened, axis=-1, keepdims=True) + EPSILON)
    ).astype(jnp.bfloat16)
    segment = doc_ids[0]
    doc_table = doc_adapter[0, :, 0]
    token_adapter = jnp.sum(
        jnp.where(
            segment[:, None] == jnp.arange(doc_table.shape[0])[None, :], doc_table[None, :], 0
        ),
        axis=1,
    )
    adapters_total = adapter_up.shape[0]
    lanes = jnp.arange(adapters_total * R)[None, :]
    own_lane = token_adapter[:, None] == lanes // R
    every_rank = lax.dot_general(
        normed,
        down_all.reshape(adapters_total * R, -1),
        (((1,), (1,)), ((), ())),
        preferred_element_type=jnp.float32,
    )
    spread = jnp.where(own_lane, every_rank, 0.0).astype(jnp.bfloat16)
    up = adapter_up.reshape(adapters_total * R, -1)

    def project(start, stop):
        base = jnp.dot(normed, qkv_all[:, start:stop], preferred_element_type=jnp.float32)
        lowrank = jnp.dot(spread, up[:, start:stop], preferred_element_type=jnp.float32)
        return (base + lowrank).astype(jnp.bfloat16)

    heads_local = width_local // HD
    cache = project(width_local, 3 * width_local)
    queries = project(0, width_local)
    positions = jnp.arange(tokens)
    allowed = (segment[:, None] == segment[None, :]) & (positions[None, :] <= positions[:, None])
    parts = []
    for head in range(heads_local):
        at = head * HD
        query = queries[:, at : at + HD]
        key = cache[:, at : at + HD]
        value = cache[:, width_local + at : width_local + at + HD]
        scores = lax.dot_general(
            query, key, (((1,), (1,)), ((), ())), preferred_element_type=jnp.float32
        ) / math.sqrt(HD)
        scores = jnp.where(allowed, scores, -1e30)
        highest = jnp.max(scores, axis=-1, keepdims=True)
        weights = jnp.exp(scores - highest)
        weights = (weights / jnp.sum(weights, axis=-1, keepdims=True)).astype(jnp.bfloat16)
        parts.append(jnp.dot(weights, value, preferred_element_type=jnp.float32).astype(jnp.bfloat16))
    attended = gather_tokens(jnp.concatenate(parts, axis=1))
    depth = depth_static[None, :] + jnp.tanh(
        jnp.dot(normed, depth_dir, preferred_element_type=jnp.float32)
    )
    new_streams = finish(stream_mixing, attended, out_all, depth, streams)

    outgoing = pack(placement, cache.reshape(page_count, PAGE, 2 * width_local), groups * capacity)
    incoming = lax.all_to_all(outgoing, "req", split_axis=0, concat_axis=0, tiled=True)
    kv_pool = unpack(chosen, incoming).reshape(page_count, PAGE, 2, width_local)
    return (new_streams, kv_pool)


def solution(mesh):
    in_specs = (
        P(None, "req", "wt"),
        P("req", None),
        P("req", None, None),
        P(),
        P(),
        P(),
        P(),
        P("req", None, "wt"),
        P("wt", None, None),
        P(None, None, None, "wt"),
        P("req", "wt"),
        P("req"),
    )
    out_specs = (P(None, "req", "wt"), P("req", None, None, "wt"))
    return jax.shard_map(body, mesh=mesh, in_specs=in_specs, out_specs=out_specs, check_vma=False)
```

```python
import functools
import math

import jax
import jax.numpy as jnp
from jax import lax
from jax.experimental import pallas as pl
from jax.experimental.pallas import tpu as pltpu
from jax.sharding import PartitionSpec as P

HD = 128
R = 16
PAGE = 16
NX, NZ, NC, NY = 4, 8, 2, 8

EPSILON = 1e-05
MESH = pl.DeviceIdType.MESH


class Copies:
    def __init__(self, send_sem, recv_sem):
        self.send_sem, self.recv_sem = send_sem, recv_sem
        self.count = 0
        self.started = []

    def start(self, src, dst, req, wt):
        index = self.count
        self.count += 1
        copy = pltpu.make_async_remote_copy(
            src_ref=src,
            dst_ref=dst,
            send_sem=self.send_sem.at[index],
            recv_sem=self.recv_sem.at[index],
            device_id=(req, wt),
            device_id_type=MESH,
        )
        copy.start()
        self.started.append(copy)
        return copy

    def finish(self):
        for copy in self.started:
            copy.wait_send()


def position():
    req = lax.axis_index("req")
    wt = lax.axis_index("wt")
    core = lax.rem(req, NC)
    z = lax.rem(req // NC, NZ)
    x = req // (NC * NZ)
    return req, wt, x, z, core


def turn(value, shift, size):
    return lax.rem(value + (shift + size), size)


def meet(partners):
    barrier = pltpu.get_barrier_semaphore()
    for req, wt in partners:
        pl.semaphore_signal(barrier, inc=1, device_id=(req, wt), device_id_type=MESH)
    pl.semaphore_wait(barrier, len(partners))


def columns(ref, half, origin):
    rows = ref.shape[0] // 2
    width = ref.shape[1] // NY
    return ref.at[pl.ds(half * rows, rows), pl.ds(pl.multiple_of(origin * width, width), width)]


def token_hop(copies, held, own, out, req, wt, half, direction, step):
    if step == 3 and half != (0 if direction == 1 else 1):
        return
    key = (half, direction)
    if step > 0:
        held[key].wait_recv()
    origin = turn(wt, -direction * step, NY)
    rows = out.shape[0] // 2
    src = own.at[pl.ds(half * rows, rows)] if step == 0 else columns(out, half, origin)
    held[key] = copies.start(src, columns(out, half, origin), req, turn(wt, direction, NY))


def gather_kernel(
    mixed, rows, out_rows, down, mixed_all, rows_all, out_all, down_all, send_sem, recv_sem, local_sem
):
    req, wt, x, z, core = position()
    partner = req + 1 - 2 * core

    def at(x_at, z_at):
        return (x_at * NZ + z_at) * NC + core

    def near_x(shift):
        return at(turn(x, shift, NX), z)

    def near_z(shift):
        return at(x, turn(z, shift, NZ))

    meet(
        [(partner, wt)]
        + [(req, turn(wt, shift, NY)) for shift in range(1, NY)]
        + [(near_z(shift), wt) for shift in range(1, NZ)]
        + [(near_x(shift), wt) for shift in range(1, NX)]
    )
    copies = Copies(send_sem, recv_sem)
    held_tokens, held_rows = {}, {}
    slice_width = down.shape[2] // NX
    both = (1, -1)

    def down_lanes(x_at):
        return pl.ds(pl.multiple_of(x_at * slice_width, slice_width), slice_width)

    def rows_hop(unit, step):
        for direction in both:
            if step == 3 and unit % 2 != (0 if direction == 1 else 1):
                continue
            key = (unit, direction)
            if step > 0:
                held_rows[key].wait_recv()
            block = rows_all.at[turn(x, -unit, NX), turn(z, -direction * step, NZ), core]
            src = rows if (step == 0 and unit == 0) else block
            held_rows[key] = copies.start(src, block, near_z(direction), wt)

    def token_step(half, step):
        for direction in both:
            token_hop(copies, held_tokens, mixed, mixed_all, req, wt, half, direction, step)

    def share(z_shift):
        block = rows_all.at[:, turn(z, z_shift, NZ), core]
        return copies.start(block, block, partner, wt)

    own_rows = rows_all.at[x, z, core]
    own_out = out_all.at[x, z, core]
    own_down = down_all.at[wt, core, :, down_lanes(x)]
    small = []
    for shift in (1, 7, 2, 6, 3, 5, 4):
        small.append(copies.start(out_rows, own_out, near_z(shift), wt))
        small.append(copies.start(down.at[core, :, down_lanes(x)], own_down, req, turn(wt, shift, NY)))
    along_x = {shift: copies.start(rows, own_rows, near_x(shift), wt) for shift in (1, 3, 2)}
    token_step(0, 0)
    rows_hop(0, 0)
    token_step(1, 0)
    half = mixed.shape[0] // 2
    locals_ = [
        pltpu.make_async_copy(rows, own_rows, local_sem.at[0]),
        pltpu.make_async_copy(mixed.at[pl.ds(0, half)], columns(mixed_all, 0, wt), local_sem.at[1]),
        pltpu.make_async_copy(mixed.at[pl.ds(half, half)], columns(mixed_all, 1, wt), local_sem.at[2]),
        pltpu.make_async_copy(down.at[core, :, down_lanes(x)], own_down, local_sem.at[3]),
        pltpu.make_async_copy(out_rows, own_out, local_sem.at[4]),
    ]
    for copy in locals_:
        copy.start()
    for shift in (1, 3, 2):
        along_x[shift].wait_recv()
        rows_hop(shift, 0)
    for copy in locals_:
        copy.wait()
    shared = [share(0)]
    rows_hop(0, 1)
    for copy in small:
        copy.wait_recv()
    down_block, out_block = down_all.at[:, core, :, down_lanes(x)], out_all.at[x, :, core]
    small = []
    for shift in (1, 3, 2):
        for block in (down_block, out_block):
            small.append(copies.start(block, block, near_x(shift), wt))
    for unit in (1, 3, 2):
        rows_hop(unit, 1)
    shared += [share(-1), share(1)]
    token_step(0, 1)
    rows_hop(0, 2)
    rows_hop(1, 2)
    token_step(1, 1)
    rows_hop(3, 2)
    rows_hop(2, 2)
    shared += [share(-2), share(2)]
    rows_hop(0, 3)
    token_step(0, 2)
    rows_hop(1, 3)
    rows_hop(3, 3)
    token_step(1, 2)
    rows_hop(2, 3)
    for copy in small:
        copy.wait_recv()
    for block in (down_all.at[:, core], out_all.at[:, :, core]):
        shared.append(copies.start(block, block, partner, wt))
    token_step(0, 3)
    for key in ((1, 1), (3, 1), (0, -1), (2, -1)):
        held_rows[key].wait_recv()
    shared += [share(-3), share(3)]
    for key in ((0, 1), (2, 1), (1, -1), (3, -1)):
        held_rows[key].wait_recv()
    shared.append(share(4))
    token_step(1, 3)
    for half in (0, 1):
        for direction in both:
            held_tokens[(half, direction)].wait_recv()
    for copy in shared:
        copy.wait_recv()
    copies.finish()


def tokens_kernel(own, out, send_sem, recv_sem, local_sem):
    req, wt, _, _, _ = position()
    meet([(req, turn(wt, 1, NY)), (req, turn(wt, -1, NY))])
    copies = Copies(send_sem, recv_sem)
    held = {}
    rows = own.shape[0] // 2
    locals_ = []
    for step in range(4):
        for half in (0, 1):
            for direction in (1, -1):
                token_hop(copies, held, own, out, req, wt, half, direction, step)
            if step == 0:
                locals_.append(
                    pltpu.make_async_copy(own.at[pl.ds(half * rows, rows)], columns(out, half, wt), local_sem.at[half])
                )
                locals_[-1].start()
    for half in (0, 1):
        for direction in (1, -1):
            held[(half, direction)].wait_recv()
    for copy in locals_:
        copy.wait()
    copies.finish()


def spec(space):
    return pl.BlockSpec(memory_space=space)


def gather_all(mixed, rows, out_rows, down):
    tokens, width = mixed.shape
    count = 3 + 28 + 8 + 14 + 2 * (7 + 3 + 1)
    return pl.pallas_call(
        gather_kernel,
        out_shape=[
            jax.ShapeDtypeStruct((tokens, width * NY), mixed.dtype),
            jax.ShapeDtypeStruct((NX, NZ, NC) + rows.shape, rows.dtype),
            jax.ShapeDtypeStruct((NX, NZ, NC) + out_rows.shape, out_rows.dtype),
            jax.ShapeDtypeStruct((NY,) + down.shape, down.dtype),
        ],
        in_specs=[spec(pltpu.VMEM)] * 4,
        out_specs=[spec(pl.ANY)] * 4,
        scratch_shapes=[
            pltpu.SemaphoreType.DMA((count,)),
            pltpu.SemaphoreType.DMA((count,)),
            pltpu.SemaphoreType.DMA((5,)),
        ],
        compiler_params=pltpu.CompilerParams(collective_id=0, has_side_effects=True),
    )(mixed, rows, out_rows, down)


def mixed_kernel(weights, streams, out):
    total = weights[0] * streams[0].astype(jnp.float32)
    for stream in range(1, streams.shape[0]):
        total = total + weights[stream] * streams[stream].astype(jnp.float32)
    out[...] = total.astype(out.dtype)


def mix_in(width_weights, streams):
    count, tokens, width = streams.shape
    block = tokens // 2
    return pl.pallas_call(
        mixed_kernel,
        grid=(tokens // block,),
        out_shape=jax.ShapeDtypeStruct((tokens, width), streams.dtype),
        in_specs=[spec(pltpu.SMEM), pl.BlockSpec((count, block, width), lambda i: (0, i, 0))],
        out_specs=pl.BlockSpec((block, width), lambda i: (i, 0)),
    )(width_weights, streams)


def pack_kernel(placement, cache, out, sem):
    started = []
    for page in range(cache.shape[0]):
        started.append(pltpu.make_async_copy(cache.at[page], out.at[placement[page]], sem.at[page]))
        started[-1].start()
    for copy in started:
        copy.wait()


def pack(placement, cache, slots):
    return pl.pallas_call(
        pack_kernel,
        out_shape=jax.ShapeDtypeStruct((slots,) + cache.shape[1:], cache.dtype),
        in_specs=[spec(pltpu.SMEM), spec(pltpu.VMEM)],
        out_specs=spec(pl.ANY),
        scratch_shapes=[pltpu.SemaphoreType.DMA((cache.shape[0],))],
    )(placement, cache)


def unpack_kernel(chosen, incoming, out):
    for page in range(out.shape[0]):
        out[page] = incoming[chosen[page]]


def unpack(chosen, incoming):
    pages = chosen.shape[0]
    return pl.pallas_call(
        unpack_kernel,
        out_shape=jax.ShapeDtypeStruct((pages,) + incoming.shape[1:], incoming.dtype),
        in_specs=[spec(pltpu.SMEM), spec(pltpu.VMEM)],
        out_specs=spec(pltpu.VMEM),
    )(chosen, incoming)


def finish_kernel(mixing, attended, weight, depth, streams, out):
    layer_out = jnp.dot(attended[...], weight[...], preferred_element_type=jnp.float32)
    count = streams.shape[0]
    wide = [streams[source].astype(jnp.float32) for source in range(count)]
    for stream in range(count):
        carried = mixing[stream, 0] * wide[0]
        for source in range(1, count):
            carried = carried + mixing[stream, source] * wide[source]
        out[stream] = (carried + depth[:, stream : stream + 1] * layer_out).astype(out.dtype)


def finish(stream_mixing, attended, weight, depth, streams):
    count, tokens, width = streams.shape
    block = tokens // 4
    return pl.pallas_call(
        finish_kernel,
        grid=(tokens // block,),
        out_shape=jax.ShapeDtypeStruct(streams.shape, streams.dtype),
        in_specs=[
            spec(pltpu.SMEM),
            pl.BlockSpec((block, attended.shape[1]), lambda i: (i, 0)),
            pl.BlockSpec(weight.shape, lambda i: (0, 0)),
            pl.BlockSpec((block, count), lambda i: (i, 0)),
            pl.BlockSpec((count, block, width), lambda i: (0, i, 0)),
        ],
        out_specs=pl.BlockSpec((count, block, width), lambda i: (0, i, 0)),
        cost_estimate=pl.CostEstimate(flops=600_000_000, bytes_accessed=6_000_000, transcendentals=0),
    )(stream_mixing, attended, weight, depth, streams)


def gather_tokens(own):
    tokens, width = own.shape
    return pl.pallas_call(
        tokens_kernel,
        out_shape=jax.ShapeDtypeStruct((tokens, width * NY), own.dtype),
        in_specs=[spec(pltpu.VMEM)],
        out_specs=spec(pl.ANY),
        scratch_shapes=[
            pltpu.SemaphoreType.DMA((14,)),
            pltpu.SemaphoreType.DMA((14,)),
            pltpu.SemaphoreType.DMA((2,)),
        ],
        compiler_params=pltpu.CompilerParams(
            collective_id=1, has_side_effects=True, vmem_limit_bytes=66_000_000
        ),
        cost_estimate=pl.CostEstimate(flops=0, bytes_accessed=60_000_000, transcendentals=0),
    )(own)


def body(
    streams,
    doc_ids,
    doc_adapter,
    width_weights,
    stream_mixing,
    depth_static,
    depth_dir,
    qkv_weight,
    adapter_down,
    adapter_up,
    out_weight,
    page_slot,
):
    count_streams = streams.shape[0]
    tokens = streams.shape[1]
    page_count = page_slot.shape[0]
    width_local = qkv_weight.shape[2]
    rows_local = qkv_weight.shape[0]
    groups = lax.axis_size("req")
    target_dev = page_slot // page_count
    local_slot = page_slot % page_count
    capacity = 2 * max(1, page_count // (2 * groups))
    ordinal = jnp.arange(page_count)
    earlier = (target_dev[None, :] == target_dev[:, None]) & (ordinal[None, :] < ordinal[:, None])
    place = jnp.sum(earlier.astype(jnp.int32), axis=1)
    placement = target_dev * capacity + place
    lane = jnp.arange(128)[None, :]
    labels = jnp.where(
        lane == 0,
        target_dev[:, None],
        jnp.where(lane == 1, local_slot[:, None], jnp.where(lane == 2, place[:, None], 0)),
    ).astype(jnp.bfloat16)
    rows = jnp.concatenate([qkv_weight.reshape(rows_local, 3 * width_local), labels], axis=1)
    gathered, rows_all, out_all, down_all = gather_all(
        mix_in(width_weights, streams), rows, out_weight, adapter_down.transpose(0, 2, 1)
    )
    rows_all = rows_all.reshape(groups * rows_local, -1)
    out_all = out_all.reshape(groups * rows_local, width_local)
    qkv_all = rows_all[:, : 3 * width_local]
    label_all = rows_all[:, 3 * width_local : 3 * width_local + 3].astype(jnp.int32)
    came = label_all[:, 0] == lax.axis_index("req")
    came_row = (jnp.arange(groups * page_count) // page_count) * capacity + label_all[:, 2]
    chosen = jnp.sum(
        jnp.where(came[None, :] & (label_all[:, 1][None, :] == ordinal[:, None]), came_row[None, :], 0), axis=1
    )

    widened = gathered.astype(jnp.float32)
    normed = (
        widened * lax.rsqrt(jnp.mean(widened * widened, axis=-1, keepdims=True) + EPSILON)
    ).astype(jnp.bfloat16)
    segment = doc_ids[0]
    doc_table = doc_adapter[0, :, 0]
    token_adapter = jnp.sum(
        jnp.where(
            segment[:, None] == jnp.arange(doc_table.shape[0])[None, :], doc_table[None, :], 0
        ),
        axis=1,
    )
    adapters_total = adapter_up.shape[0]
    lanes = jnp.arange(adapters_total * R)[None, :]
    own_lane = token_adapter[:, None] == lanes // R
    every_rank = lax.dot_general(
        normed,
        down_all.reshape(adapters_total * R, -1),
        (((1,), (1,)), ((), ())),
        preferred_element_type=jnp.float32,
    )
    spread = jnp.where(own_lane, every_rank, 0.0).astype(jnp.bfloat16)
    up = adapter_up.reshape(adapters_total * R, -1)

    def project(start, stop):
        base = jnp.dot(normed, qkv_all[:, start:stop], preferred_element_type=jnp.float32)
        lowrank = jnp.dot(spread, up[:, start:stop], preferred_element_type=jnp.float32)
        return (base + lowrank).astype(jnp.bfloat16)

    heads_local = width_local // HD
    cache = project(width_local, 3 * width_local)
    queries = project(0, width_local)
    positions = jnp.arange(tokens)
    allowed = (segment[:, None] == segment[None, :]) & (positions[None, :] <= positions[:, None])
    parts = []
    for head in range(heads_local):
        at = head * HD
        query = queries[:, at : at + HD]
        key = cache[:, at : at + HD]
        value = cache[:, width_local + at : width_local + at + HD]
        scores = lax.dot_general(
            query, key, (((1,), (1,)), ((), ())), preferred_element_type=jnp.float32
        ) / math.sqrt(HD)
        scores = jnp.where(allowed, scores, -1e30)
        highest = jnp.max(scores, axis=-1, keepdims=True)
        weights = jnp.exp(scores - highest)
        weights = (weights / jnp.sum(weights, axis=-1, keepdims=True)).astype(jnp.bfloat16)
        parts.append(jnp.dot(weights, value, preferred_element_type=jnp.float32).astype(jnp.bfloat16))
    attended = gather_tokens(jnp.concatenate(parts, axis=1))
    depth = depth_static[None, :] + jnp.tanh(
        jnp.dot(normed, depth_dir, preferred_element_type=jnp.float32)
    )
    new_streams = finish(stream_mixing, attended, out_all, depth, streams)

    outgoing = pack(placement, cache.reshape(page_count, PAGE, 2 * width_local), groups * capacity)
    incoming = lax.all_to_all(outgoing, "req", split_axis=0, concat_axis=0, tiled=True)
    kv_pool = unpack(chosen, incoming).reshape(page_count, PAGE, 2, width_local)
    return (new_streams, kv_pool)


def solution(mesh):
    in_specs = (
        P(None, "req", "wt"),
        P("req", None),
        P("req", None, None),
        P(),
        P(),
        P(),
        P(),
        P("req", None, "wt"),
        P("wt", None, None),
        P(None, None, None, "wt"),
        P("req", "wt"),
        P("req"),
    )
    out_specs = (P(None, "req", "wt"), P("req", None, None, "wt"))
    return jax.shard_map(body, mesh=mesh, in_specs=in_specs, out_specs=out_specs, check_vma=False)
```
